32 devices in a mesh: groups: 2 (over x), tiles: 16 (over z, y, core).
Axes of the slice: x: 2, y: 2, z: 4, core: 2. Of those that a mesh axis runs over, the one named last changes fastest.
Arguments:
- features: bfloat16 [512, 128, 128], P(('groups', 'tiles')), parts along dimension 0, may hold values from -40 to 40
- window_offsets: int32 [4], P('groups'), parts along dimension 0, may hold values from 0 to 31
- self_project: bfloat16 [128, 384], replicated, may hold values from -0.5 to 0.5
- self_merge: bfloat16 [128, 128], replicated, may hold values from -0.5 to 0.5
- cross_project: bfloat16 [128, 384], replicated, may hold values from -0.5 to 0.5
- cross_merge: bfloat16 [128, 128], replicated, may hold values from -0.5 to 0.5
- feed_in: bfloat16 [256, 512], replicated, may hold values from -0.375 to 0.375
- feed_out: bfloat16 [512, 128], replicated, may hold values from -0.25 to 0.25
- norm_gains: float32 [3, 128], replicated, may hold values from 0.1 to 1.9
- result_grad: float32 [512, 128, 128], P(('groups', 'tiles')), parts along dimension 0, may hold values from -6 to 6
Outputs:
- result: bfloat16 [512, 128, 128], P(('groups', 'tiles')), parts along dimension 0
- features_grad: float32 [512, 128, 128], P(('groups', 'tiles')), parts along dimension 0
- self_project_grad: float32 [256, 384], P(('groups', 'tiles')), parts along dimension 0
- self_merge_grad: float32 [256, 128], P(('groups', 'tiles')), parts along dimension 0
- cross_project_grad: float32 [256, 384], P(('groups', 'tiles')), parts along dimension 0
- cross_merge_grad: float32 [256, 128], P(('groups', 'tiles')), parts along dimension 0
- feed_in_grad: float32 [512, 512], P(('groups', 'tiles')), parts along dimension 0
- feed_out_grad: float32 [1024, 128], P(('groups', 'tiles')), parts along dimension 0
- norm_gains_grad: float32 [6, 128], P('groups', 'tiles'), parts along dimension 0
The draws below stay inside these ranges and needn't reach their ends.
There are 2 independent parts, one for each index of `groups`. The reference program is written for one: setup_inputs(seed, part) draws one part's arguments, and reference() takes and returns one part's arrays. A program takes and returns all parts, laid end to end along the dimension named above; an argument that names none is the same for every part. Nothing has to cross between parts.
All inputs are finite; a program needn't handle non-finite values.
Results may differ from the reference program's by a relative error of at most 0.017.
The reference program's roundings to bfloat16 on the way count: a program that leaves them out, or rounds other values in their place, can miss the bound.
Values may be sent and summed in bfloat16 or wider, within the bound.
No kernel may reach another device: no remote copies, remote signals or barrier semaphores. Data moves between devices by JAX's collectives and lax.ppermute only.
A program may use at most 128 MiB of HBM per device.

```python
import jax
import jax.numpy as jnp
from jax import lax

D = 128
FF = 512
HT = 16
WD = 128
WIN = 32
ROWS = 256
N_TILES = 16


def draw_features(key, part):
    base_key = jax.random.fold_in(jax.random.fold_in(key, 71), 0)
    values = jax.random.normal(base_key, (ROWS, WD, D), jnp.float32)
    return jnp.clip(values, -40.0, 40.0).astype(jnp.bfloat16)


def block_scale(key, dims, cuts, smallest, largest):
    def one(dim, shards_of):
        draws = jax.random.uniform(jax.random.fold_in(jax.random.fold_in(key, 6), dim), (shards_of,), jnp.float32, smallest / len(cuts), largest / len(cuts))
        return jnp.repeat(jnp.exp(draws), dims[dim] // shards_of).reshape((-1,) + (1,) * (len(dims) - dim - 1))

    factor_of = one(*cuts[0])
    for cut in cuts[1:]:
        factor_of = factor_of * one(*cut)
    return factor_of


def bell_draw(stream_key, extent, scale, reach, cuts=(), kind=jnp.bfloat16):
    drawn = jax.random.normal(stream_key, extent, jnp.float32) * scale
    if len(cuts) > 0:
        drawn = block_scale(stream_key, extent, cuts, -0.22, 0.18) * drawn
    return jnp.clip(drawn, min=-reach, max=reach).astype(kind)


def setup_inputs(seed: int = 0, part: int = 0) -> dict:
    streams_of = jax.random.split(jax.random.key(seed), 11)
    own_keys = jax.random.split(jax.random.fold_in(streams_of[10], part), 11)
    features = draw_features(jax.random.fold_in(jax.random.fold_in(streams_of[10], part), 71), part)
    window_offsets = jax.random.randint(own_keys[1], (2,), 0, WIN).astype(jnp.int32)
    self_project = bell_draw(streams_of[2], (D, 3 * D), D ** -0.5, 0.5)
    self_merge = bell_draw(streams_of[3], (D, D), D ** -0.5, 0.5)
    cross_project = bell_draw(streams_of[4], (D, 3 * D), D ** -0.5, 0.5)
    cross_merge = bell_draw(streams_of[5], (D, D), D ** -0.5, 0.5)
    feed_in = bell_draw(streams_of[6], (2 * D, FF), (2 * D) ** -0.5, 0.375)
    feed_out = bell_draw(streams_of[7], (FF, D), FF ** -0.5, 0.25)
    norm_gains = jnp.clip(1.0 + 0.18 * jax.random.normal(streams_of[8], (3, D), jnp.float32), 0.1, 1.9)
    result_grad = bell_draw(own_keys[9], (ROWS, WD, D), 1.0, 6.0, ((0, 16),), jnp.float32)
    return {"features": features, "window_offsets": window_offsets, "self_project": self_project, "self_merge": self_merge, "cross_project": cross_project, "cross_merge": cross_merge, "feed_in": feed_in, "feed_out": feed_out, "norm_gains": norm_gains, "result_grad": result_grad}


NORM_EPS = 1e-05
MASK_FILL = -1000000000.0
HALF_ROOT = 0.7071067811865476
DENSITY_COEF = 0.3989422804014327

def project(inputs, weight):
    return jnp.dot(inputs, weight, preferred_element_type=jnp.float32)

def back_project(grad_rows, weight):
    return jnp.dot(grad_rows, weight.T, preferred_element_type=jnp.float32)

def weight_grad(inputs, grad_rows):
    return jnp.dot(inputs.T, grad_rows, preferred_element_type=jnp.float32)

def layer_norm(values, norm_gain):
    center = values - lax.optimization_barrier(jnp.mean(values, axis=-1, keepdims=True))
    inverse = lax.rsqrt(lax.optimization_barrier(jnp.mean(center * center, axis=-1, keepdims=True)) + NORM_EPS)
    unit_rows = center * inverse
    return (unit_rows * norm_gain, unit_rows, inverse)

def norm_backward(upstream, norm_gain, unit_rows, inverse):
    scaled = upstream * norm_gain
    value_gradient = inverse * (scaled - lax.optimization_barrier(jnp.mean(scaled, axis=-1, keepdims=True)) - unit_rows * lax.optimization_barrier(jnp.mean(scaled * unit_rows, axis=-1, keepdims=True)))
    return (value_gradient, lax.optimization_barrier(jnp.sum(upstream * unit_rows, axis=0)))

def gelu_exact(values):
    return 0.5 * values * (1.0 + lax.erf(values * HALF_ROOT))

def gelu_slope(values):
    return 0.5 * (1.0 + lax.erf(values * HALF_ROOT)) + values * jnp.exp(-0.5 * values * values) * DENSITY_COEF

def to_windows(array, row_groups, group_rows, col_groups):
    width = array.shape[-1]
    shaped = array.reshape(row_groups, group_rows, col_groups, WIN, width)
    return shaped.transpose(0, 2, 1, 3, 4).reshape(row_groups * col_groups, group_rows * WIN, width)

def from_windows(array, row_groups, group_rows, col_groups):
    width = array.shape[-1]
    shaped = array.reshape(row_groups, col_groups, group_rows, WIN, width)
    return shaped.transpose(0, 2, 1, 3, 4).reshape(row_groups * group_rows, col_groups * WIN, width)

def attention_shares(query_rows, key_matrix, key_valid, logit_scale):
    attention_logits = jnp.einsum('hcn,hzn->hcz', query_rows.astype(jnp.float32), key_matrix.astype(jnp.float32)) * logit_scale
    attention_logits = jnp.where(key_valid, attention_logits, MASK_FILL)
    top_score = lax.optimization_barrier(jnp.max(attention_logits, axis=-1, keepdims=True))
    raised = jnp.exp(attention_logits - top_score)
    shares = raised / lax.optimization_barrier(jnp.sum(raised, axis=-1, keepdims=True))
    return (shares, shares.astype(jnp.bfloat16))

def apply_shares(portion_weights, value_matrix):
    return jnp.einsum('tni,tip->tnp', portion_weights.astype(jnp.float32), value_matrix.astype(jnp.float32)).astype(jnp.bfloat16)

def shares_backward(query_rows, key_matrix, value_matrix, shares, portion_weights, mixture_gradient, logit_scale):
    float_gradient = mixture_gradient.astype(jnp.float32)
    portion_gradient = jnp.einsum('hcn,hzn->hcz', float_gradient, value_matrix.astype(jnp.float32))
    value_gradient = jnp.einsum('nvw,nvc->nwc', portion_weights.astype(jnp.float32), float_gradient)
    inner_sum = lax.optimization_barrier(jnp.sum(portion_gradient * shares, axis=-1, keepdims=True))
    logit_gradient = (shares * (portion_gradient - inner_sum) * logit_scale).astype(jnp.bfloat16).astype(jnp.float32)
    query_gradient = jnp.einsum('tni,tip->tnp', logit_gradient, key_matrix.astype(jnp.float32))
    key_gradient = jnp.einsum('nvw,nvc->nwc', logit_gradient, query_rows.astype(jnp.float32))
    return (query_gradient, key_gradient, value_gradient)

def window_layout(image_rows):
    half_rows = HT // 2
    row_groups = image_rows // HT + 1
    col_groups = WD // WIN
    row_index = jnp.arange(row_groups * HT)
    row_flags = (row_index >= half_rows) & (row_index < half_rows + image_rows)
    key_valid = jnp.broadcast_to(row_flags.reshape(row_groups, 1, HT, 1), (row_groups, col_groups, HT, WIN)).reshape(row_groups * col_groups, 1, HT * WIN)
    return (half_rows, row_groups, col_groups, key_valid)

def self_forward(one_image, offset, self_project):
    image_rows = one_image.shape[0]
    half_rows, row_groups, col_groups, key_valid = window_layout(image_rows)
    rolled = jnp.roll(one_image, -offset, axis=1)
    projected = project(rolled.reshape(-1, D), self_project).astype(jnp.bfloat16).reshape(image_rows, WD, 3 * D)
    padded = jnp.pad(projected, ((half_rows, half_rows), (0, 0), (0, 0)))
    windows = to_windows(padded, row_groups, HT, col_groups)
    shares, portion_weights = attention_shares(windows[:, :, :D], windows[:, :, D:2 * D], key_valid, D ** (-0.5))
    mixed = apply_shares(portion_weights, windows[:, :, 2 * D:])
    mixed_rows = from_windows(mixed, row_groups, HT, col_groups)[half_rows:half_rows + image_rows]
    return (jnp.roll(mixed_rows, offset, axis=1), rolled, windows, shares, portion_weights)

def self_backward(mixture_gradient, offset, windows, shares, portion_weights):
    image_rows = mixture_gradient.shape[0]
    half_rows, row_groups, col_groups, key_valid = window_layout(image_rows)
    rolled_grad = jnp.roll(mixture_gradient, -offset, axis=1)
    padded = jnp.pad(rolled_grad, ((half_rows, half_rows), (0, 0), (0, 0)))
    grad_windows = to_windows(padded, row_groups, HT, col_groups)
    query_gradient, key_gradient, value_gradient = shares_backward(windows[:, :, :D], windows[:, :, D:2 * D], windows[:, :, 2 * D:], shares, portion_weights, grad_windows, D ** (-0.5))
    combined = jnp.concatenate([query_gradient, key_gradient, value_gradient], axis=-1)
    grad_rows = from_windows(combined, row_groups, HT, col_groups)[half_rows:half_rows + image_rows]
    return grad_rows.astype(jnp.bfloat16)

def reference(features, window_offsets, self_project, self_merge, cross_project, cross_merge, feed_in, feed_out, norm_gains, result_grad):
    half_tiles = N_TILES // 2
    quarter_rows = N_TILES // 4 * HT
    image_rows = half_tiles * HT
    tile_tokens = HT * WD
    all_tokens = 2 * image_rows * WD
    logit_scale = D ** (-0.5)
    grad_scale = all_tokens ** (-0.5)
    features = jnp.roll(features, -quarter_rows, axis=0)
    result_grad = jnp.roll(result_grad, -quarter_rows, axis=0)
    flat_features = features.reshape(all_tokens, D)
    mix_list = []
    rolled_list = []
    saved_list = []
    for image_index in range(2):
        one_image = features[image_index * image_rows:(image_index + 1) * image_rows]
        mixed, rolled, windows, shares, portion_weights = self_forward(one_image, window_offsets[image_index], self_project)
        mix_list.append(mixed)
        rolled_list.append(rolled.reshape(-1, D))
        saved_list.append((windows, shares, portion_weights))
    self_mix = jnp.concatenate(mix_list, axis=0).reshape(all_tokens, D)
    rolled_flat = jnp.concatenate(rolled_list, axis=0)
    self_normed, self_unit, self_inverse = layer_norm(project(self_mix, self_merge), norm_gains[0])
    middle = (flat_features.astype(jnp.float32) + self_normed).astype(jnp.bfloat16)
    cross_query = project(middle, cross_project[:, :D]).astype(jnp.bfloat16)
    cross_keyval = project(middle, cross_project[:, D:]).astype(jnp.bfloat16)
    query_tiles = cross_query.reshape(2 * half_tiles, tile_tokens, D)
    keyval_tiles = cross_keyval.reshape(2, half_tiles, tile_tokens, 2 * D)[::-1].reshape(2 * half_tiles, tile_tokens, 2 * D)
    all_valid = jnp.ones((1, 1, tile_tokens), dtype=jnp.bool_)

    def cross_tile(pieces):
        query_tile, keyval_tile = pieces
        shares, portion_weights = attention_shares(query_tile[None], keyval_tile[None, :, :D], all_valid, logit_scale)
        return apply_shares(portion_weights, keyval_tile[None, :, D:])[0]
    cross_mix = lax.map(cross_tile, (query_tiles, keyval_tiles)).reshape(all_tokens, D)
    cross_full, cross_unit, cross_inverse = layer_norm(project(cross_mix, cross_merge), norm_gains[1])
    cross_normed = cross_full.astype(jnp.bfloat16)
    joined = jnp.concatenate([middle, cross_normed], axis=1)
    feed_pre = project(joined, feed_in)
    feed_hidden = gelu_exact(feed_pre).astype(jnp.bfloat16)
    feed_normed, feed_unit, feed_inverse = layer_norm(project(feed_hidden, feed_out), norm_gains[2])
    result = (middle.astype(jnp.float32) + feed_normed).astype(jnp.bfloat16)
    upstream = result_grad.reshape(all_tokens, D)
    grad_post_full, gain_feed = norm_backward(upstream, norm_gains[2], feed_unit, feed_inverse)
    grad_post = grad_post_full.astype(jnp.bfloat16)
    grad_pre = (back_project(grad_post, feed_out) * gelu_slope(feed_pre)).astype(jnp.bfloat16)
    grad_joined = back_project(grad_pre, feed_in)
    feed_in_grad = weight_grad(joined, grad_pre) * grad_scale
    feed_out_grad = weight_grad(feed_hidden, grad_post) * grad_scale
    grad_cross_full, gain_cross = norm_backward(grad_joined[:, D:], norm_gains[1], cross_unit, cross_inverse)
    grad_cross_merged = grad_cross_full.astype(jnp.bfloat16)
    cross_merge_grad = weight_grad(cross_mix, grad_cross_merged) * grad_scale
    grad_cross_mix = back_project(grad_cross_merged, cross_merge).astype(jnp.bfloat16)

    def cross_tile_back(pieces):
        query_tile, keyval_tile, grad_tile = pieces
        shares, portion_weights = attention_shares(query_tile[None], keyval_tile[None, :, :D], all_valid, logit_scale)
        query_gradient, key_gradient, value_gradient = shares_backward(query_tile[None], keyval_tile[None, :, :D], keyval_tile[None, :, D:], shares, portion_weights, grad_tile[None], logit_scale)
        return (query_gradient[0].astype(jnp.bfloat16), jnp.concatenate([key_gradient[0], value_gradient[0]], axis=-1).astype(jnp.bfloat16))
    grad_query_tiles, grad_keyval_tiles = lax.map(cross_tile_back, (query_tiles, keyval_tiles, grad_cross_mix.reshape(2 * half_tiles, tile_tokens, D)))
    grad_cross_query = grad_query_tiles.reshape(all_tokens, D)
    returned_keyval = grad_keyval_tiles.reshape(2, half_tiles, tile_tokens, 2 * D)[::-1].reshape(all_tokens, 2 * D)
    grad_middle = upstream + grad_joined[:, :D] + back_project(grad_cross_query, cross_project[:, :D]) + back_project(returned_keyval, cross_project[:, D:])
    cross_project_grad = jnp.concatenate([weight_grad(middle, grad_cross_query), weight_grad(middle, returned_keyval)], axis=1) * grad_scale
    grad_self_full, gain_self = norm_backward(grad_middle, norm_gains[0], self_unit, self_inverse)
    grad_self_merged = grad_self_full.astype(jnp.bfloat16)
    self_merge_grad = weight_grad(self_mix, grad_self_merged) * grad_scale
    grad_self_mix = back_project(grad_self_merged, self_merge).astype(jnp.bfloat16).reshape(2, image_rows, WD, D)
    proj_grads = []
    feature_terms = []
    for image_index in range(2):
        windows, shares, portion_weights = saved_list[image_index]
        grad_rows = self_backward(grad_self_mix[image_index], window_offsets[image_index], windows, shares, portion_weights)
        flat_grad = grad_rows.reshape(-1, 3 * D)
        proj_grads.append(flat_grad)
        term = back_project(flat_grad, self_project).reshape(image_rows, WD, D)
        feature_terms.append(jnp.roll(term, window_offsets[image_index], axis=1))
    grad_self_proj = jnp.concatenate(proj_grads, axis=0)
    self_project_grad = weight_grad(rolled_flat, grad_self_proj) * grad_scale
    features_grad = grad_middle.reshape(2 * image_rows, WD, D) + jnp.concatenate(feature_terms, axis=0)
    norm_gains_grad = jnp.stack([gain_self, gain_cross, gain_feed], axis=0) * grad_scale
    result_rows = jnp.roll(result.reshape(2 * image_rows, WD, D), quarter_rows, axis=0)
    features_grad = jnp.roll(features_grad, quarter_rows, axis=0)
    return (result_rows, features_grad, self_project_grad, self_merge_grad, cross_project_grad, cross_merge_grad, feed_in_grad, feed_out_grad, norm_gains_grad)
```

```python
import functools
import math

import jax
import jax.numpy as jnp
from jax import lax
from jax.experimental import pallas as pl
from jax.experimental.pallas import tpu as pltpu
from jax.sharding import PartitionSpec as P

D = 128
WIN = 32

NORM_EPS = 1e-05
MASK_FILL = -1000000000.0
HALF_ROOT = 0.7071067811865476
DENSITY_COEF = 0.3989422804014327
LOG2_E = 1.4426950408889634
SCALE = D ** (-0.5)


F32 = jnp.float32
BF16 = jnp.bfloat16


def dot_nn(a, b):
    return lax.dot_general(a, b, (((1,), (0,)), ((), ())), preferred_element_type=F32)


def dot_nt(a, b):
    return lax.dot_general(a, b, (((1,), (1,)), ((), ())), preferred_element_type=F32)


def dot_tn(a, b):
    return lax.dot_general(a, b, (((0,), (0,)), ((), ())), preferred_element_type=F32)


def layer_norm(values, gain):
    center = values - jnp.mean(values, axis=-1, keepdims=True)
    inverse = lax.rsqrt(jnp.mean(center * center, axis=-1, keepdims=True) + NORM_EPS)
    unit = center * inverse
    return unit * gain, unit, inverse


def norm_backward(upstream, gain, unit, inverse):
    scaled = upstream * gain
    grad = inverse * (
        scaled
        - jnp.mean(scaled, axis=-1, keepdims=True)
        - unit * jnp.mean(scaled * unit, axis=-1, keepdims=True)
    )
    return grad, jnp.sum(upstream * unit, axis=0, keepdims=True)


def roll_matrices(offset, size):
    i = lax.broadcasted_iota(jnp.int32, (size, size), 0)
    j = lax.broadcasted_iota(jnp.int32, (size, size), 1)
    row_source = i + offset
    row_source = jnp.where(row_source >= size, row_source - size, row_source)
    col_source = j + offset
    col_source = jnp.where(col_source >= size, col_source - size, col_source)
    forward = jnp.where(j == row_source, 1.0, 0.0).astype(BF16)
    back = jnp.where(i == col_source, 1.0, 0.0).astype(BF16)
    return forward, back


def pick(ref, cols, lanes):
    block = ref[:, cols, lanes]
    return block.reshape(block.shape[0] * block.shape[1], block.shape[2])


def self_forward_kernel(
    scal_ref, own_ref, halo_ref, project_ref, merge_ref, gains_ref,
    middle_ref, mix_ref, qkv_ref, halo_kv_ref, own_rolled, halo_rolled, mix_rolled,
    *, valid_slot,
):
    rows, cols = own_ref.shape[0], own_ref.shape[1]
    forward, back = roll_matrices(scal_ref[0], cols)
    valid = scal_ref[valid_slot] > 0
    for r in range(rows):
        own_rolled[r] = dot_nn(forward, own_ref[r]).astype(BF16)
        halo_rolled[r] = dot_nn(forward, halo_ref[r]).astype(BF16)
    tokens = rows * cols
    qkv_ref[...] = (
        dot_nn(own_rolled[...].reshape(tokens, D), project_ref[...])
        .astype(BF16).reshape(rows, cols, 3 * D)
    )
    halo_kv_ref[...] = (
        dot_nn(halo_rolled[...].reshape(tokens, D), project_ref[:, D:])
        .astype(BF16).reshape(rows, cols, 2 * D)
    )
    for w in range(cols // WIN):
        span = slice(w * WIN, (w + 1) * WIN)
        q = pick(qkv_ref, span, slice(0, D))
        s_own = dot_nt(q, pick(qkv_ref, span, slice(D, 2 * D))) * SCALE
        s_halo = dot_nt(q, pick(halo_kv_ref, span, slice(0, D))) * SCALE
        s_halo = jnp.where(valid, s_halo, MASK_FILL)
        top = jnp.maximum(
            jnp.max(s_own, axis=-1, keepdims=True), jnp.max(s_halo, axis=-1, keepdims=True)
        )
        p_own = jnp.exp(s_own - top)
        p_halo = jnp.exp(s_halo - top)
        inv = 1.0 / (
            jnp.sum(p_own, axis=-1, keepdims=True) + jnp.sum(p_halo, axis=-1, keepdims=True)
        )
        mixed = dot_nn(
            (p_own * inv).astype(BF16), pick(qkv_ref, span, slice(2 * D, 3 * D))
        ) + dot_nn((p_halo * inv).astype(BF16), pick(halo_kv_ref, span, slice(D, 2 * D)))
        mix_rolled[:, span, :] = mixed.astype(BF16).reshape(rows, WIN, D)
    for r in range(rows):
        mix_ref[r * cols : (r + 1) * cols, :] = dot_nn(back, mix_rolled[r]).astype(BF16)
    normed, _, _ = layer_norm(dot_nn(mix_ref[...], merge_ref[...]), gains_ref[0:1, :])
    middle_ref[...] = (own_ref[...].reshape(tokens, D).astype(F32) + normed).astype(BF16)


def full_spec(shape):
    zeros = (0,) * len(shape)
    return pl.BlockSpec(shape, lambda *_: zeros)


def self_forward(group, scal, features, halo, self_project, self_merge, norm_gains):
    rows, cols, _ = halo.shape
    tokens = rows * cols
    return pl.pallas_call(
        functools.partial(self_forward_kernel, valid_slot=1 + group),
        grid=(1,),
        in_specs=[
            pl.BlockSpec(memory_space=pltpu.SMEM),
            pl.BlockSpec((rows, cols, D), lambda i: (group, 0, 0)),
            full_spec(halo.shape),
            full_spec(self_project.shape),
            full_spec(self_merge.shape),
            full_spec(norm_gains.shape),
        ],
        out_specs=[
            full_spec((tokens, D)),
            full_spec((tokens, D)),
            full_spec((rows, cols, 3 * D)),
            full_spec((rows, cols, 2 * D)),
        ],
        out_shape=[
            jax.ShapeDtypeStruct((tokens, D), BF16),
            jax.ShapeDtypeStruct((tokens, D), BF16),
            jax.ShapeDtypeStruct((rows, cols, 3 * D), BF16),
            jax.ShapeDtypeStruct((rows, cols, 2 * D), BF16),
        ],
        scratch_shapes=[pltpu.VMEM((rows, cols, D), BF16)] * 3,
        name="self_forward",
    )(scal, features, halo, self_project, self_merge, norm_gains)


def cross_open_kernel(middle_ref, partner_ref, project_ref, q_ref, kv_ref, mix_ref, stat_ref):
    @pl.when(pl.program_id(0) == 0)
    def _():
        kv_ref[...] = dot_nn(partner_ref[...], project_ref[:, D:]).astype(BF16)

    q = dot_nn(middle_ref[...], project_ref[:, :D]).astype(BF16)
    q_ref[...] = q
    logits = dot_nt(q, kv_ref[:, :D]) * (SCALE * LOG2_E)
    top = jnp.max(logits, axis=-1, keepdims=True)
    raised = jnp.exp2(logits - top)
    total = jnp.sum(raised, axis=-1, keepdims=True)
    mix_ref[...] = dot_nn(raised.astype(BF16), kv_ref[:, D:])
    lane = lax.broadcasted_iota(jnp.int32, stat_ref.shape, 1)
    stat_ref[...] = jnp.where(lane == 0, top, total)


def cross_open(block, middles, partner, cross_project):
    chunk = partner.shape[0]
    tokens = middles.shape[0]
    row = lambda i: (i, 0)
    return pl.pallas_call(
        cross_open_kernel,
        grid=(tokens // block,),
        in_specs=[
            pl.BlockSpec((block, D), row),
            full_spec(partner.shape),
            full_spec(cross_project.shape),
        ],
        out_specs=[
            pl.BlockSpec((block, D), row),
            full_spec((chunk, 2 * D)),
            pl.BlockSpec((block, D), row),
            pl.BlockSpec((block, D), row),
        ],
        out_shape=[
            jax.ShapeDtypeStruct((tokens, D), BF16),
            jax.ShapeDtypeStruct((chunk, 2 * D), BF16),
            jax.ShapeDtypeStruct((tokens, D), F32),
            jax.ShapeDtypeStruct((tokens, D), F32),
        ],
        name="cross_open",
    )(middles, partner, cross_project)


def cross_close_kernel(
    middle_ref, partner_ref, project_ref, q_ref, open_mix_ref, open_stat_ref,
    merge_ref, feed_in_ref, feed_out_ref, gains_ref, upstream_ref,
    kv_ref, result_ref, mid_grad_ref, mix_grad_ref, stat_ref,
    grad_in_ref, grad_out_ref, grad_merge_ref, grad_gain_ref,
):
    @pl.when(pl.program_id(0) == 0)
    def _():
        kv_ref[...] = dot_nn(partner_ref[...], project_ref[:, D:]).astype(BF16)
        grad_in_ref[...] = jnp.zeros_like(grad_in_ref)
        grad_out_ref[...] = jnp.zeros_like(grad_out_ref)
        grad_merge_ref[...] = jnp.zeros_like(grad_merge_ref)
        grad_gain_ref[...] = jnp.zeros_like(grad_gain_ref)

    block = middle_ref.shape[0]
    logits = dot_nt(q_ref[...], kv_ref[:, :D]) * (SCALE * LOG2_E)
    open_top = open_stat_ref[:, 0:1]
    open_total = open_stat_ref[:, 1:2]
    top = jnp.maximum(jnp.max(logits, axis=-1, keepdims=True), open_top)
    raised = jnp.exp2(logits - top)
    carry = jnp.exp2(open_top - top)
    total = jnp.sum(raised, axis=-1, keepdims=True) + open_total * carry
    mixed = dot_nn(raised.astype(BF16), kv_ref[:, D:]) + open_mix_ref[...] * carry
    mixed = mixed * (1.0 / total)
    log_total = top + jnp.log2(total)
    cross_mix = mixed.astype(BF16)

    middle = middle_ref[...]
    gain_cross = gains_ref[1:2, :]
    gain_feed = gains_ref[2:3, :]
    cross_full, cross_unit, cross_inverse = layer_norm(
        dot_nn(cross_mix, merge_ref[...]), gain_cross
    )
    cross_normed = cross_full.astype(BF16)
    feed_pre = dot_nn(middle, feed_in_ref[:D, :]) + dot_nn(cross_normed, feed_in_ref[D:, :])
    bell = 0.5 * (1.0 + lax.erf(feed_pre * HALF_ROOT))
    hidden = (feed_pre * bell).astype(BF16)
    slope = bell + feed_pre * (jnp.exp(-0.5 * feed_pre * feed_pre) * DENSITY_COEF)
    feed_normed, feed_unit, feed_inverse = layer_norm(
        dot_nn(hidden, feed_out_ref[...]), gain_feed
    )
    result_ref[...] = (middle.astype(F32) + feed_normed).astype(BF16)
    upstream = upstream_ref[...]
    post_full, gain_grad_feed = norm_backward(upstream, gain_feed, feed_unit, feed_inverse)
    grad_post = post_full.astype(BF16)
    grad_pre = (dot_nt(grad_post, feed_out_ref[...]) * slope).astype(BF16)
    grad_joined = dot_nt(grad_pre, feed_in_ref[...])
    mid_grad_ref[...] = upstream + grad_joined[:, :D]
    lanes = grad_in_ref.shape[0]
    grad_low = dot_tn(middle, grad_pre)
    grad_high = dot_tn(cross_normed, grad_pre)
    for b in range(lanes):
        grad_in_ref[b, :D, :] += grad_low[:, b * D : (b + 1) * D]
        grad_in_ref[b, D:, :] += grad_high[:, b * D : (b + 1) * D]
    grad_out_ref[...] += dot_tn(hidden, grad_post)
    merged_full, gain_grad_cross = norm_backward(
        grad_joined[:, D:], gain_cross, cross_unit, cross_inverse
    )
    grad_merged = merged_full.astype(BF16)
    grad_merge_ref[...] += dot_tn(cross_mix, grad_merged)
    mix_grad = dot_nt(grad_merged, merge_ref[...]).astype(BF16)
    mix_grad_ref[...] = mix_grad
    inner = jnp.sum(mix_grad.astype(F32) * mixed, axis=-1, keepdims=True)
    lane = lax.broadcasted_iota(jnp.int32, (block, D), 1)
    stats = jnp.where(lane == 0, log_total, inner)
    stat_ref[...] = stats.T[: stat_ref.shape[0], :]
    grad_gain_ref[1:2, :] += gain_grad_cross
    grad_gain_ref[2:3, :] += gain_grad_feed


def cross_close(
    block, middles, partner, cross_project, q, open_mix, open_stat,
    cross_merge, feed_in, feed_out, norm_gains, upstream,
):
    tokens = middles.shape[0]
    chunk = partner.shape[0]
    hidden = feed_in.shape[1]
    row = lambda i: (i, 0)
    tile = pl.BlockSpec((block, D), row)
    return pl.pallas_call(
        cross_close_kernel,
        grid=(tokens // block,),
        in_specs=[
            tile, full_spec(partner.shape), full_spec(cross_project.shape), tile, tile, tile,
            full_spec(cross_merge.shape), full_spec(feed_in.shape), full_spec(feed_out.shape),
            full_spec(norm_gains.shape), tile,
        ],
        out_specs=[
            full_spec((chunk, 2 * D)), tile, tile, tile,
            pl.BlockSpec((8, block), lambda i: (0, i)),
            full_spec((hidden // D, 2 * D, D)), full_spec((hidden, D)), full_spec((D, D)),
            full_spec((8, D)),
        ],
        out_shape=[
            jax.ShapeDtypeStruct((chunk, 2 * D), BF16),
            jax.ShapeDtypeStruct((tokens, D), BF16),
            jax.ShapeDtypeStruct((tokens, D), F32),
            jax.ShapeDtypeStruct((tokens, D), BF16),
            jax.ShapeDtypeStruct((8, tokens), F32),
            jax.ShapeDtypeStruct((hidden // D, 2 * D, D), F32),
            jax.ShapeDtypeStruct((hidden, D), F32),
            jax.ShapeDtypeStruct((D, D), F32),
            jax.ShapeDtypeStruct((8, D), F32),
        ],
        name="cross_close",
    )(middles, partner, cross_project, q, open_mix, open_stat,
      cross_merge, feed_in, feed_out, norm_gains, upstream)


def cross_back_kernel(*refs, first, last, q_block):
    refs = list(refs)
    q_ref, grad_ref, stat_ref, kv_ref, partner_ref, project_ref = refs[:6]
    refs = refs[6:]
    if not first:
        q_in_ref, weight_in_ref = refs[:2]
        refs = refs[2:]
    if last:
        mid_grad_ref, middle_ref = refs[:2]
        refs = refs[2:]
    term_ref, q_out_ref, weight_ref, k_acc, v_acc, q_acc = refs
    step = pl.program_id(0)

    @pl.when(step == 0)
    def _():
        if first:
            q_acc[...] = jnp.zeros_like(q_acc)
            weight_ref[...] = jnp.zeros_like(weight_ref)
        else:
            q_acc[...] = q_in_ref[...]
            weight_ref[...] = weight_in_ref[...]

    k_acc[...] = jnp.zeros_like(k_acc)
    v_acc[...] = jnp.zeros_like(v_acc)
    keys = kv_ref[:, :D]
    values = kv_ref[:, D:]
    tokens = q_ref.shape[0]

    @pl.loop(0, tokens // q_block)
    def _(j):
        span = pl.ds(pl.multiple_of(j * q_block, q_block), q_block)
        q = q_ref[span, :]
        grad = grad_ref[span, :]
        log_total = stat_ref[0:1, span]
        inner = stat_ref[1:2, span]
        shares = jnp.exp2(dot_nt(keys, q) * (SCALE * LOG2_E) - log_total)
        slopes = dot_nt(values, grad) - inner
        v_acc[...] += dot_nn(shares.astype(BF16), grad)
        logit_grad = (shares * slopes).astype(BF16)
        k_acc[...] += dot_nn(logit_grad, q)
        q_acc[span, :] += dot_tn(logit_grad, keys)

    pair = jnp.concatenate(
        [(k_acc[...] * SCALE).astype(BF16), v_acc[...].astype(BF16)], axis=1
    )
    term_ref[...] = dot_nt(pair, project_ref[:, D:]).astype(BF16)
    pair_weight = dot_tn(partner_ref[...], pair)
    weight_ref[1] += pair_weight[:, :D]
    weight_ref[2] += pair_weight[:, D:]

    @pl.when(step == pl.num_programs(0) - 1)
    def _():
        if last:
            q_grad = (q_acc[...] * SCALE).astype(BF16)
            q_out_ref[...] = mid_grad_ref[...] + dot_nt(q_grad, project_ref[:, :D])
            weight_ref[0] += dot_tn(middle_ref[...], q_grad)
        else:
            q_out_ref[...] = q_acc[...]


def cross_back(
    block, q_block, q, mix_grad, stats, kv, partner, cross_project, carried=None, finish=None
):
    tokens = q.shape[0]
    chunk = kv.shape[0]
    first, last = carried is None, finish is not None
    args = [q, mix_grad, stats, kv, partner, cross_project]
    specs = [
        full_spec(q.shape), full_spec(mix_grad.shape), full_spec(stats.shape),
        pl.BlockSpec((block, 2 * D), lambda i: (i, 0)),
        pl.BlockSpec((block, D), lambda i: (i, 0)),
        full_spec(cross_project.shape),
    ]
    for extra in (carried or ()) + (finish or ()):
        args.append(extra)
        specs.append(full_spec(extra.shape))
    return pl.pallas_call(
        functools.partial(cross_back_kernel, first=first, last=last, q_block=q_block),
        grid=(chunk // block,),
        in_specs=specs,
        out_specs=[
            pl.BlockSpec((block, D), lambda i: (i, 0)),
            full_spec((tokens, D)), full_spec((3, D, D)),
        ],
        out_shape=[
            jax.ShapeDtypeStruct((chunk, D), BF16),
            jax.ShapeDtypeStruct((tokens, D), F32),
            jax.ShapeDtypeStruct((3, D, D), F32),
        ],
        scratch_shapes=[
            pltpu.VMEM((block, D), F32), pltpu.VMEM((block, D), F32), pltpu.VMEM((tokens, D), F32)
        ],
        name="cross_back",
    )(*args)


def self_back_kernel(
    scal_ref, own_ref, halo_ref, qkv_ref, halo_kv_ref, mix_ref, mid_grad_ref, term_ref,
    project_ref, merge_ref, gains_ref,
    feature_grad_ref, halo_term_ref, weight_ref, merge_grad_ref, gain_ref,
    mix_grad, own_grad, halo_grad, own_back, halo_back,
    *, valid_slot,
):
    rows, cols = own_ref.shape[0], own_ref.shape[1]
    tokens = rows * cols
    forward, back = roll_matrices(scal_ref[0], cols)
    valid = scal_ref[valid_slot] > 0
    upstream = mid_grad_ref[...] + term_ref[...].astype(F32)
    gain = gains_ref[0:1, :]
    _, unit, inverse = layer_norm(dot_nn(mix_ref[...], merge_ref[...]), gain)
    merged_full, gain_grad = norm_backward(upstream, gain, unit, inverse)
    gain_ref[...] = jnp.broadcast_to(gain_grad, gain_ref.shape)
    grad_merged = merged_full.astype(BF16)
    merge_grad_ref[...] = dot_tn(mix_ref[...], grad_merged)
    plain_grad = dot_nt(grad_merged, merge_ref[...]).astype(BF16)
    for r in range(rows):
        mix_grad[r] = dot_nn(forward, plain_grad[r * cols : (r + 1) * cols, :]).astype(BF16)
    for w in range(cols // WIN):
        span = slice(w * WIN, (w + 1) * WIN)
        q = pick(qkv_ref, span, slice(0, D))
        k_own = pick(qkv_ref, span, slice(D, 2 * D))
        k_halo = pick(halo_kv_ref, span, slice(0, D))
        grad = pick(mix_grad, span, slice(0, D))
        s_own = dot_nt(k_own, q) * SCALE
        s_halo = jnp.where(valid, dot_nt(k_halo, q) * SCALE, MASK_FILL)
        top = jnp.maximum(
            jnp.max(s_own, axis=0, keepdims=True), jnp.max(s_halo, axis=0, keepdims=True)
        )
        p_own = jnp.exp(s_own - top)
        p_halo = jnp.exp(s_halo - top)
        inv = 1.0 / (
            jnp.sum(p_own, axis=0, keepdims=True) + jnp.sum(p_halo, axis=0, keepdims=True)
        )
        p_own = p_own * inv
        p_halo = p_halo * inv
        d_own = dot_nt(pick(qkv_ref, span, slice(2 * D, 3 * D)), grad)
        d_halo = dot_nt(pick(halo_kv_ref, span, slice(D, 2 * D)), grad)
        inner = jnp.sum(p_own * d_own, axis=0, keepdims=True) + jnp.sum(
            p_halo * d_halo, axis=0, keepdims=True
        )
        l_own = (p_own * (d_own - inner) * SCALE).astype(BF16)
        l_halo = (p_halo * (d_halo - inner) * SCALE).astype(BF16)
        q_grad = dot_tn(l_own, k_own) + dot_tn(l_halo, k_halo)
        shape = (rows, WIN, D)
        own_grad[:, span, :D] = q_grad.astype(BF16).reshape(shape)
        own_grad[:, span, D : 2 * D] = dot_nn(l_own, q).astype(BF16).reshape(shape)
        own_grad[:, span, 2 * D :] = dot_nn(p_own.astype(BF16), grad).astype(BF16).reshape(shape)
        halo_grad[:, span, :D] = dot_nn(l_halo, q).astype(BF16).reshape(shape)
        halo_grad[:, span, D:] = dot_nn(p_halo.astype(BF16), grad).astype(BF16).reshape(shape)
    for r in range(rows):
        line = slice(r * cols, (r + 1) * cols)
        halo_back[line, :] = dot_nn(back, halo_grad[r]).astype(BF16)
        own_back[line, :] = dot_nn(back, own_grad[r]).astype(BF16)
    halo_term_ref[...] = dot_nt(halo_back[...], project_ref[:, D:]).astype(BF16)
    feature_grad_ref[...] = upstream + dot_nt(own_back[...], project_ref[...])
    own = own_ref[...].reshape(tokens, D)
    halo = halo_ref[...].reshape(tokens, D)
    own_weight = dot_tn(own, own_back[...])
    halo_weight = dot_tn(halo, halo_back[...])
    weight_ref[0] = own_weight[:, :D]
    weight_ref[1] = own_weight[:, D : 2 * D] + halo_weight[:, :D]
    weight_ref[2] = own_weight[:, 2 * D :] + halo_weight[:, D:]


def self_back(
    group, scal, features, halo, qkv, halo_kv, mix, mid_grad, term,
    self_project, self_merge, norm_gains,
):
    rows, cols, _ = halo.shape
    tokens = rows * cols
    return pl.pallas_call(
        functools.partial(self_back_kernel, valid_slot=1 + group),
        grid=(1,),
        in_specs=[
            pl.BlockSpec(memory_space=pltpu.SMEM),
            pl.BlockSpec((rows, cols, D), lambda i: (group, 0, 0)),
            full_spec(halo.shape), full_spec(qkv.shape), full_spec(halo_kv.shape),
            full_spec(mix.shape),
            pl.BlockSpec((tokens, D), lambda i: (group, 0)),
            full_spec(term.shape),
            full_spec(self_project.shape), full_spec(self_merge.shape),
            full_spec(norm_gains.shape),
        ],
        out_specs=[
            full_spec((tokens, D)), full_spec((tokens, D)), full_spec((3, D, D)),
            full_spec((D, D)), full_spec((8, D)),
        ],
        out_shape=[
            jax.ShapeDtypeStruct((tokens, D), F32),
            jax.ShapeDtypeStruct((tokens, D), BF16),
            jax.ShapeDtypeStruct((3, D, D), F32),
            jax.ShapeDtypeStruct((D, D), F32),
            jax.ShapeDtypeStruct((8, D), F32),
        ],
        scratch_shapes=[
            pltpu.VMEM((rows, cols, D), BF16),
            pltpu.VMEM((rows, cols, 3 * D), BF16),
            pltpu.VMEM((rows, cols, 2 * D), BF16),
            pltpu.VMEM((tokens, 3 * D), BF16),
            pltpu.VMEM((tokens, 2 * D), BF16),
        ],
        name="self_back",
    )(scal, features, halo, qkv, halo_kv, mix, mid_grad, term,
      self_project, self_merge, norm_gains)


def scattered_sum(pieces, axis):
    count = lax.axis_size(axis)
    place = lax.axis_index(axis)
    current = pieces
    bit = 1
    while bit < count:
        pairs = current.reshape((current.shape[0] // 2, 2) + current.shape[1:])
        odd = (place & bit) != 0
        kept = jnp.where(odd, pairs[:, 1], pairs[:, 0])
        sent = jnp.where(odd, pairs[:, 0], pairs[:, 1]).astype(BF16)
        got = lax.ppermute(sent, axis, [(i, i ^ bit) for i in range(count)])
        current = kept + got.astype(F32)
        bit *= 2
    return current[0]


def body(
    features, window_offsets, self_project, self_merge, cross_project, cross_merge,
    feed_in, feed_out, norm_gains, result_grad,
):
    tile_rows, tile_cols = features.shape[0], features.shape[1]
    half_rows = tile_rows // 2
    tile_tokens = tile_rows * tile_cols
    half_tokens = tile_tokens // 2
    count = lax.axis_size("tiles")
    half_tiles = count // 2
    shift = count // 4
    position = lax.axis_index("tiles")
    image_place = (position + count - shift) % count
    offset = window_offsets[image_place // half_tiles]
    grad_scale = 1.0 / math.sqrt(count * tile_tokens)
    upper_valid = image_place % half_tiles != 0
    lower_valid = image_place % half_tiles != half_tiles - 1
    scal = jnp.stack(
        [offset, upper_valid.astype(jnp.int32), lower_valid.astype(jnp.int32)]
    )
    inner = [
        ((i + shift) % count, (i + 1 + shift) % count)
        for i in range(count)
        if i % half_tiles != half_tiles - 1
    ]
    to_next = inner
    to_previous = [(b, a) for a, b in inner]
    to_partner = [(i, (i + half_tiles) % count) for i in range(count)]

    halos = (
        lax.ppermute(features[half_rows:], "tiles", to_next),
        lax.ppermute(features[:half_rows], "tiles", to_previous),
    )
    parts = [
        self_forward(g, scal, features, halos[g], self_project, self_merge, norm_gains)
        for g in range(2)
    ]
    partners = [lax.ppermute(parts[g][0], "tiles", to_partner) for g in range(2)]
    middles = jnp.concatenate([parts[0][0], parts[1][0]], axis=0)

    block = min(512, half_tokens)
    upstream = result_grad.reshape(tile_tokens, D)
    q, kv_a, open_mix, open_stat = cross_open(block, middles, partners[0], cross_project)
    (kv_b, result, mid_grad, mix_grad, stats, grad_in, grad_out, grad_merge, gain_grad) = (
        cross_close(
            block, middles, partners[1], cross_project, q, open_mix, open_stat,
            cross_merge, feed_in, feed_out, norm_gains, upstream,
        )
    )
    term_a, q_grad, weight_a = cross_back(
        block, block, q, mix_grad, stats, kv_a, partners[0], cross_project
    )
    got_a = lax.ppermute(term_a, "tiles", to_partner)
    term_b, mid_grad, cross_weight = cross_back(
        block, block, q, mix_grad, stats, kv_b, partners[1], cross_project,
        carried=(q_grad, weight_a), finish=(mid_grad, middles),
    )
    got_b = lax.ppermute(term_b, "tiles", to_partner)
    backs = [
        self_back(
            g, scal, features, halos[g], parts[g][2], parts[g][3], parts[g][1], mid_grad,
            (got_a, got_b)[g], self_project, self_merge, norm_gains,
        )
        for g in range(2)
    ]
    from_next = lax.ppermute(backs[0][1], "tiles", to_previous)
    from_previous = lax.ppermute(backs[1][1], "tiles", to_next)
    features_grad = jnp.concatenate(
        [
            backs[0][0] + from_previous.astype(F32),
            backs[1][0] + from_next.astype(F32),
        ],
        axis=0,
    ).reshape(tile_rows, tile_cols, D)

    self_weight = backs[0][2] + backs[1][2]
    merge_weight = backs[0][3] + backs[1][3]
    gains = jnp.concatenate(
        [backs[0][4][0:1] + backs[1][4][0:1], gain_grad[1:8]], axis=0
    )

    def cut(array):
        return array.reshape(count, array.shape[0] // count, D)

    summed = scattered_sum(
        jnp.concatenate(
            [cut(self_weight[b]) for b in range(3)]
            + [cut(merge_weight)]
            + [cut(cross_weight[b]) for b in range(3)]
            + [cut(grad_merge)]
            + [cut(grad_in[b]) for b in range(grad_in.shape[0])]
            + [cut(grad_out)]
            + [jnp.broadcast_to(gains[None], (count,) + gains.shape)],
            axis=1,
        ),
        "tiles",
    ) * grad_scale
    place = 0

    def take(rows, blocks):
        nonlocal place
        found = [summed[place + b * rows : place + (b + 1) * rows] for b in range(blocks)]
        place += rows * blocks
        return jnp.concatenate(found, axis=1)

    out_self = take(D // count, 3)
    out_self_merge = take(D // count, 1)
    out_cross = take(D // count, 3)
    out_cross_merge = take(D // count, 1)
    out_in = take(2 * D // count, feed_in.shape[1] // D)
    out_out = take(feed_out.shape[0] // count, 1)
    lanes = D // count
    out_gains = lax.dynamic_slice(summed[place : place + 3], (0, position * lanes), (3, lanes))
    return (
        result.reshape(tile_rows, tile_cols, D),
        features_grad,
        out_self,
        out_self_merge,
        out_cross,
        out_cross_merge,
        out_in,
        out_out,
        out_gains,
    )


def solution(mesh):
    whole = P(("groups", "tiles"), None, None)
    rows = P(("groups", "tiles"), None)
    return jax.shard_map(
        body,
        mesh=mesh,
        in_specs=(whole, P("groups"), P(), P(), P(), P(), P(), P(), P(), whole),
        out_specs=(whole, whole, rows, rows, rows, rows, rows, rows, P("groups", "tiles")),
        check_vma=False,
    )
```

```python
import functools
import math

import jax
import jax.numpy as jnp
from jax import lax
from jax.experimental import pallas as pl
from jax.experimental.pallas import tpu as pltpu
from jax.sharding import PartitionSpec as P


D = 128
WIN = 32

NORM_EPS = 1e-05
MASK_FILL = -1000000000.0
HALF_ROOT = 0.7071067811865476
DENSITY_COEF = 0.3989422804014327
LOG2_E = 1.4426950408889634
SCALE = D ** (-0.5)


F32 = jnp.float32
BF16 = jnp.bfloat16


def dot_nn(a, b):
    return lax.dot_general(a, b, (((1,), (0,)), ((), ())), preferred_element_type=F32)


def dot_nt(a, b):
    return lax.dot_general(a, b, (((1,), (1,)), ((), ())), preferred_element_type=F32)


def dot_tn(a, b):
    return lax.dot_general(a, b, (((0,), (0,)), ((), ())), preferred_element_type=F32)


def layer_norm(values, gain):
    center = values - jnp.mean(values, axis=-1, keepdims=True)
    inverse = lax.rsqrt(jnp.mean(center * center, axis=-1, keepdims=True) + NORM_EPS)
    unit = center * inverse
    return unit * gain, unit, inverse


def norm_backward(upstream, gain, unit, inverse):
    scaled = upstream * gain
    grad = inverse * (
        scaled
        - jnp.mean(scaled, axis=-1, keepdims=True)
        - unit * jnp.mean(scaled * unit, axis=-1, keepdims=True)
    )
    return grad, jnp.sum(upstream * unit, axis=0, keepdims=True)


def roll_matrices(offset, size):
    i = lax.broadcasted_iota(jnp.int32, (size, size), 0)
    j = lax.broadcasted_iota(jnp.int32, (size, size), 1)
    row_source = i + offset
    row_source = jnp.where(row_source >= size, row_source - size, row_source)
    col_source = j + offset
    col_source = jnp.where(col_source >= size, col_source - size, col_source)
    forward = jnp.where(j == row_source, 1.0, 0.0).astype(BF16)
    back = jnp.where(i == col_source, 1.0, 0.0).astype(BF16)
    return forward, back


def pick(ref, cols, lanes):
    block = ref[:, cols, lanes]
    return block.reshape(block.shape[0] * block.shape[1], block.shape[2])


def self_forward_kernel(
    scal_ref, own_ref, halo_ref, project_ref, merge_ref, gains_ref,
    middle_ref, mix_ref, qkv_ref, halo_kv_ref, own_rolled, halo_rolled, mix_rolled,
    *, valid_slot,
):
    rows, cols = own_ref.shape[0], own_ref.shape[1]
    forward, back = roll_matrices(scal_ref[0], cols)
    valid = scal_ref[valid_slot] > 0
    for r in range(rows):
        own_rolled[r] = dot_nn(forward, own_ref[r]).astype(BF16)
        halo_rolled[r] = dot_nn(forward, halo_ref[r]).astype(BF16)
    tokens = rows * cols
    qkv_ref[...] = (
        dot_nn(own_rolled[...].reshape(tokens, D), project_ref[...])
        .astype(BF16).reshape(rows, cols, 3 * D)
    )
    halo_kv_ref[...] = (
        dot_nn(halo_rolled[...].reshape(tokens, D), project_ref[:, D:])
        .astype(BF16).reshape(rows, cols, 2 * D)
    )
    for w in range(cols // WIN):
        span = slice(w * WIN, (w + 1) * WIN)
        q = pick(qkv_ref, span, slice(0, D))
        s_own = dot_nt(q, pick(qkv_ref, span, slice(D, 2 * D))) * SCALE
        s_halo = dot_nt(q, pick(halo_kv_ref, span, slice(0, D))) * SCALE
        s_halo = jnp.where(valid, s_halo, MASK_FILL)
        top = jnp.maximum(
            jnp.max(s_own, axis=-1, keepdims=True), jnp.max(s_halo, axis=-1, keepdims=True)
        )
        p_own = jnp.exp(s_own - top)
        p_halo = jnp.exp(s_halo - top)
        inv = 1.0 / (
            jnp.sum(p_own, axis=-1, keepdims=True) + jnp.sum(p_halo, axis=-1, keepdims=True)
        )
        mixed = dot_nn(
            (p_own * inv).astype(BF16), pick(qkv_ref, span, slice(2 * D, 3 * D))
        ) + dot_nn((p_halo * inv).astype(BF16), pick(halo_kv_ref, span, slice(D, 2 * D)))
        mix_rolled[:, span, :] = mixed.astype(BF16).reshape(rows, WIN, D)
    for r in range(rows):
        mix_ref[r * cols : (r + 1) * cols, :] = dot_nn(back, mix_rolled[r]).astype(BF16)
    normed, _, _ = layer_norm(dot_nn(mix_ref[...], merge_ref[...]), gains_ref[0:1, :])
    middle_ref[...] = (own_ref[...].reshape(tokens, D).astype(F32) + normed).astype(BF16)


def full_spec(shape):
    zeros = (0,) * len(shape)
    return pl.BlockSpec(shape, lambda *_: zeros)


def self_forward(group, scal, features, halo, self_project, self_merge, norm_gains):
    rows, cols, _ = halo.shape
    tokens = rows * cols
    return pl.pallas_call(
        functools.partial(self_forward_kernel, valid_slot=1 + group),
        grid=(1,),
        in_specs=[
            pl.BlockSpec(memory_space=pltpu.SMEM),
            pl.BlockSpec((rows, cols, D), lambda i: (group, 0, 0)),
            full_spec(halo.shape),
            full_spec(self_project.shape),
            full_spec(self_merge.shape),
            full_spec(norm_gains.shape),
        ],
        out_specs=[
            full_spec((tokens, D)),
            full_spec((tokens, D)),
            full_spec((rows, cols, 3 * D)),
            full_spec((rows, cols, 2 * D)),
        ],
        out_shape=[
            jax.ShapeDtypeStruct((tokens, D), BF16),
            jax.ShapeDtypeStruct((tokens, D), BF16),
            jax.ShapeDtypeStruct((rows, cols, 3 * D), BF16),
            jax.ShapeDtypeStruct((rows, cols, 2 * D), BF16),
        ],
        scratch_shapes=[pltpu.VMEM((rows, cols, D), BF16)] * 3,
        name="self_forward",
    )(scal, features, halo, self_project, self_merge, norm_gains)


def cross_open_kernel(middle_ref, partner_ref, project_ref, q_ref, kv_ref, mix_ref, stat_ref):
    @pl.when(pl.program_id(0) == 0)
    def _():
        kv_ref[...] = dot_nn(partner_ref[...], project_ref[:, D:]).astype(BF16)

    q = dot_nn(middle_ref[...], project_ref[:, :D]).astype(BF16)
    q_ref[...] = q
    logits = dot_nt(q, kv_ref[:, :D]) * (SCALE * LOG2_E)
    top = jnp.max(logits, axis=-1, keepdims=True)
    raised = jnp.exp2(logits - top)
    total = jnp.sum(raised, axis=-1, keepdims=True)
    mix_ref[...] = dot_nn(raised.astype(BF16), kv_ref[:, D:])
    lane = lax.broadcasted_iota(jnp.int32, stat_ref.shape, 1)
    stat_ref[...] = jnp.where(lane == 0, top, total)


def cross_open(block, middles, partner, cross_project):
    chunk = partner.shape[0]
    tokens = middles.shape[0]
    row = lambda i: (i, 0)
    return pl.pallas_call(
        cross_open_kernel,
        grid=(tokens // block,),
        in_specs=[
            pl.BlockSpec((block, D), row),
            full_spec(partner.shape),
            full_spec(cross_project.shape),
        ],
        out_specs=[
            pl.BlockSpec((block, D), row),
            full_spec((chunk, 2 * D)),
            pl.BlockSpec((block, D), row),
            pl.BlockSpec((block, D), row),
        ],
        out_shape=[
            jax.ShapeDtypeStruct((tokens, D), BF16),
            jax.ShapeDtypeStruct((chunk, 2 * D), BF16),
            jax.ShapeDtypeStruct((tokens, D), F32),
            jax.ShapeDtypeStruct((tokens, D), F32),
        ],
        name="cross_open",
    )(middles, partner, cross_project)


def cross_close_kernel(
    middle_ref, partner_ref, project_ref, q_ref, open_mix_ref, open_stat_ref,
    merge_ref, feed_in_ref, feed_out_ref, gains_ref, upstream_ref,
    kv_ref, result_ref, mid_grad_ref, mix_grad_ref, stat_ref,
    grad_in_ref, grad_out_ref, grad_merge_ref, grad_gain_ref,
):
    @pl.when(pl.program_id(0) == 0)
    def _():
        kv_ref[...] = dot_nn(partner_ref[...], project_ref[:, D:]).astype(BF16)
        grad_in_ref[...] = jnp.zeros_like(grad_in_ref)
        grad_out_ref[...] = jnp.zeros_like(grad_out_ref)
        grad_merge_ref[...] = jnp.zeros_like(grad_merge_ref)
        grad_gain_ref[...] = jnp.zeros_like(grad_gain_ref)

    block = middle_ref.shape[0]
    logits = dot_nt(q_ref[...], kv_ref[:, :D]) * (SCALE * LOG2_E)
    open_top = open_stat_ref[:, 0:1]
    open_total = open_stat_ref[:, 1:2]
    top = jnp.maximum(jnp.max(logits, axis=-1, keepdims=True), open_top)
    raised = jnp.exp2(logits - top)
    carry = jnp.exp2(open_top - top)
    total = jnp.sum(raised, axis=-1, keepdims=True) + open_total * carry
    mixed = dot_nn(raised.astype(BF16), kv_ref[:, D:]) + open_mix_ref[...] * carry
    mixed = mixed * (1.0 / total)
    log_total = top + jnp.log2(total)
    cross_mix = mixed.astype(BF16)

    middle = middle_ref[...]
    gain_cross = gains_ref[1:2, :]
    gain_feed = gains_ref[2:3, :]
    cross_full, cross_unit, cross_inverse = layer_norm(
        dot_nn(cross_mix, merge_ref[...]), gain_cross
    )
    cross_normed = cross_full.astype(BF16)
    feed_pre = dot_nn(middle, feed_in_ref[:D, :]) + dot_nn(cross_normed, feed_in_ref[D:, :])
    bell = 0.5 * (1.0 + lax.erf(feed_pre * HALF_ROOT))
    hidden = (feed_pre * bell).astype(BF16)
    slope = bell + feed_pre * (jnp.exp(-0.5 * feed_pre * feed_pre) * DENSITY_COEF)
    feed_normed, feed_unit, feed_inverse = layer_norm(
        dot_nn(hidden, feed_out_ref[...]), gain_feed
    )
    result_ref[...] = (middle.astype(F32) + feed_normed).astype(BF16)
    upstream = upstream_ref[...]
    post_full, gain_grad_feed = norm_backward(upstream, gain_feed, feed_unit, feed_inverse)
    grad_post = post_full.astype(BF16)
    grad_pre = (dot_nt(grad_post, feed_out_ref[...]) * slope).astype(BF16)
    grad_joined = dot_nt(grad_pre, feed_in_ref[...])
    mid_grad_ref[...] = upstream + grad_joined[:, :D]
    lanes = grad_in_ref.shape[0]
    grad_low = dot_tn(middle, grad_pre)
    grad_high = dot_tn(cross_normed, grad_pre)
    for b in range(lanes):
        grad_in_ref[b, :D, :] += grad_low[:, b * D : (b + 1) * D]
        grad_in_ref[b, D:, :] += grad_high[:, b * D : (b + 1) * D]
    grad_out_ref[...] += dot_tn(hidden, grad_post)
    merged_full, gain_grad_cross = norm_backward(
        grad_joined[:, D:], gain_cross, cross_unit, cross_inverse
    )
    grad_merged = merged_full.astype(BF16)
    grad_merge_ref[...] += dot_tn(cross_mix, grad_merged)
    mix_grad = dot_nt(grad_merged, merge_ref[...]).astype(BF16)
    mix_grad_ref[...] = mix_grad
    inner = jnp.sum(mix_grad.astype(F32) * mixed, axis=-1, keepdims=True)
    lane = lax.broadcasted_iota(jnp.int32, (block, D), 1)
    stats = jnp.where(lane == 0, log_total, inner)
    stat_ref[...] = stats.T[: stat_ref.shape[0], :]
    grad_gain_ref[1:2, :] += gain_grad_cross
    grad_gain_ref[2:3, :] += gain_grad_feed


def cross_close(
    block, middles, partner, cross_project, q, open_mix, open_stat,
    cross_merge, feed_in, feed_out, norm_gains, upstream,
):
    tokens = middles.shape[0]
    chunk = partner.shape[0]
    hidden = feed_in.shape[1]
    row = lambda i: (i, 0)
    tile = pl.BlockSpec((block, D), row)
    return pl.pallas_call(
        cross_close_kernel,
        grid=(tokens // block,),
        in_specs=[
            tile, full_spec(partner.shape), full_spec(cross_project.shape), tile, tile, tile,
            full_spec(cross_merge.shape), full_spec(feed_in.shape), full_spec(feed_out.shape),
            full_spec(norm_gains.shape), tile,
        ],
        out_specs=[
            full_spec((chunk, 2 * D)), tile, tile, tile,
            pl.BlockSpec((8, block), lambda i: (0, i)),
            full_spec((hidden // D, 2 * D, D)), full_spec((hidden, D)), full_spec((D, D)),
            full_spec((8, D)),
        ],
        out_shape=[
            jax.ShapeDtypeStruct((chunk, 2 * D), BF16),
            jax.ShapeDtypeStruct((tokens, D), BF16),
            jax.ShapeDtypeStruct((tokens, D), F32),
            jax.ShapeDtypeStruct((tokens, D), BF16),
            jax.ShapeDtypeStruct((8, tokens), F32),
            jax.ShapeDtypeStruct((hidden // D, 2 * D, D), F32),
            jax.ShapeDtypeStruct((hidden, D), F32),
            jax.ShapeDtypeStruct((D, D), F32),
            jax.ShapeDtypeStruct((8, D), F32),
        ],
        name="cross_close",
    )(middles, partner, cross_project, q, open_mix, open_stat,
      cross_merge, feed_in, feed_out, norm_gains, upstream)


def cross_back_kernel(*refs, first, last, q_block):
    refs = list(refs)
    q_ref, grad_ref, stat_ref, kv_ref, partner_ref, project_ref = refs[:6]
    refs = refs[6:]
    if not first:
        q_in_ref, weight_in_ref = refs[:2]
        refs = refs[2:]
    if last:
        mid_grad_ref, middle_ref = refs[:2]
        refs = refs[2:]
    term_ref, q_out_ref, weight_ref, k_acc, v_acc, q_acc = refs
    step = pl.program_id(0)

    @pl.when(step == 0)
    def _():
        if first:
            q_acc[...] = jnp.zeros_like(q_acc)
            weight_ref[...] = jnp.zeros_like(weight_ref)
        else:
            q_acc[...] = q_in_ref[...]
            weight_ref[...] = weight_in_ref[...]

    k_acc[...] = jnp.zeros_like(k_acc)
    v_acc[...] = jnp.zeros_like(v_acc)
    keys = kv_ref[:, :D]
    values = kv_ref[:, D:]
    tokens = q_ref.shape[0]

    @pl.loop(0, tokens // q_block)
    def _(j):
        span = pl.ds(pl.multiple_of(j * q_block, q_block), q_block)
        q = q_ref[span, :]
        grad = grad_ref[span, :]
        log_total = stat_ref[0:1, span]
        inner = stat_ref[1:2, span]
        shares = jnp.exp2(dot_nt(keys, q) * (SCALE * LOG2_E) - log_total)
        slopes = dot_nt(values, grad) - inner
        v_acc[...] += dot_nn(shares.astype(BF16), grad)
        logit_grad = (shares * slopes).astype(BF16)
        k_acc[...] += dot_nn(logit_grad, q)
        q_acc[span, :] += dot_tn(logit_grad, keys)

    pair = jnp.concatenate(
        [(k_acc[...] * SCALE).astype(BF16), v_acc[...].astype(BF16)], axis=1
    )
    term_ref[...] = dot_nt(pair, project_ref[:, D:]).astype(BF16)
    pair_weight = dot_tn(partner_ref[...], pair)
    weight_ref[1] += pair_weight[:, :D]
    weight_ref[2] += pair_weight[:, D:]

    @pl.when(step == pl.num_programs(0) - 1)
    def _():
        if last:
            q_grad = (q_acc[...] * SCALE).astype(BF16)
            q_out_ref[...] = mid_grad_ref[...] + dot_nt(q_grad, project_ref[:, :D])
            weight_ref[0] += dot_tn(middle_ref[...], q_grad)
        else:
            q_out_ref[...] = q_acc[...]


def cross_back(
    block, index, q_block, q, mix_grad, stats, kv, partner, cross_project,
    carried=None, finish=None,
):
    tokens = q.shape[0]
    first, last = carried is None, finish is not None
    args = [q, mix_grad, stats, kv, partner, cross_project]
    specs = [
        full_spec(q.shape), full_spec(mix_grad.shape), full_spec(stats.shape),
        pl.BlockSpec((block, 2 * D), lambda i: (index, 0)),
        pl.BlockSpec((block, D), lambda i: (index, 0)),
        full_spec(cross_project.shape),
    ]
    for extra in (carried or ()) + (finish or ()):
        args.append(extra)
        specs.append(full_spec(extra.shape))
    return pl.pallas_call(
        functools.partial(cross_back_kernel, first=first, last=last, q_block=q_block),
        grid=(1,),
        in_specs=specs,
        out_specs=[
            full_spec((block, D)), full_spec((tokens, D)), full_spec((3, D, D)),
        ],
        out_shape=[
            jax.ShapeDtypeStruct((block, D), BF16),
            jax.ShapeDtypeStruct((tokens, D), F32),
            jax.ShapeDtypeStruct((3, D, D), F32),
        ],
        scratch_shapes=[
            pltpu.VMEM((block, D), F32), pltpu.VMEM((block, D), F32), pltpu.VMEM((tokens, D), F32)
        ],
        name="cross_back",
    )(*args)


def self_back_kernel(
    scal_ref, own_ref, halo_ref, qkv_ref, halo_kv_ref, mix_ref, mid_grad_ref,
    term_low_ref, term_high_ref, project_ref, merge_ref, gains_ref,
    feature_grad_ref, halo_term_ref, weight_ref, merge_grad_ref, gain_ref,
    mix_grad, own_grad, halo_grad, own_back, halo_back,
    *, valid_slot,
):
    rows, cols = own_ref.shape[0], own_ref.shape[1]
    tokens = rows * cols
    forward, back = roll_matrices(scal_ref[0], cols)
    valid = scal_ref[valid_slot] > 0
    upstream = mid_grad_ref[...] + jnp.concatenate(
        [term_low_ref[...].astype(F32), term_high_ref[...].astype(F32)], axis=0
    )
    gain = gains_ref[0:1, :]
    _, unit, inverse = layer_norm(dot_nn(mix_ref[...], merge_ref[...]), gain)
    merged_full, gain_grad = norm_backward(upstream, gain, unit, inverse)
    gain_ref[...] = jnp.broadcast_to(gain_grad, gain_ref.shape)
    grad_merged = merged_full.astype(BF16)
    merge_grad_ref[...] = dot_tn(mix_ref[...], grad_merged)
    plain_grad = dot_nt(grad_merged, merge_ref[...]).astype(BF16)
    for r in range(rows):
        mix_grad[r] = dot_nn(forward, plain_grad[r * cols : (r + 1) * cols, :]).astype(BF16)
    for w in range(cols // WIN):
        span = slice(w * WIN, (w + 1) * WIN)
        q = pick(qkv_ref, span, slice(0, D))
        k_own = pick(qkv_ref, span, slice(D, 2 * D))
        k_halo = pick(halo_kv_ref, span, slice(0, D))
        grad = pick(mix_grad, span, slice(0, D))
        s_own = dot_nt(k_own, q) * SCALE
        s_halo = jnp.where(valid, dot_nt(k_halo, q) * SCALE, MASK_FILL)
        top = jnp.maximum(
            jnp.max(s_own, axis=0, keepdims=True), jnp.max(s_halo, axis=0, keepdims=True)
        )
        p_own = jnp.exp(s_own - top)
        p_halo = jnp.exp(s_halo - top)
        inv = 1.0 / (
            jnp.sum(p_own, axis=0, keepdims=True) + jnp.sum(p_halo, axis=0, keepdims=True)
        )
        p_own = p_own * inv
        p_halo = p_halo * inv
        d_own = dot_nt(pick(qkv_ref, span, slice(2 * D, 3 * D)), grad)
        d_halo = dot_nt(pick(halo_kv_ref, span, slice(D, 2 * D)), grad)
        inner = jnp.sum(p_own * d_own, axis=0, keepdims=True) + jnp.sum(
            p_halo * d_halo, axis=0, keepdims=True
        )
        l_own = (p_own * (d_own - inner) * SCALE).astype(BF16)
        l_halo = (p_halo * (d_halo - inner) * SCALE).astype(BF16)
        q_grad = dot_tn(l_own, k_own) + dot_tn(l_halo, k_halo)
        shape = (rows, WIN, D)
        own_grad[:, span, :D] = q_grad.astype(BF16).reshape(shape)
        own_grad[:, span, D : 2 * D] = dot_nn(l_own, q).astype(BF16).reshape(shape)
        own_grad[:, span, 2 * D :] = dot_nn(p_own.astype(BF16), grad).astype(BF16).reshape(shape)
        halo_grad[:, span, :D] = dot_nn(l_halo, q).astype(BF16).reshape(shape)
        halo_grad[:, span, D:] = dot_nn(p_halo.astype(BF16), grad).astype(BF16).reshape(shape)
    for r in range(rows):
        line = slice(r * cols, (r + 1) * cols)
        halo_back[line, :] = dot_nn(back, halo_grad[r]).astype(BF16)
        own_back[line, :] = dot_nn(back, own_grad[r]).astype(BF16)
    halo_term_ref[...] = dot_nt(halo_back[...], project_ref[:, D:]).astype(BF16)
    feature_grad_ref[...] = upstream + dot_nt(own_back[...], project_ref[...])
    own = own_ref[...].reshape(tokens, D)
    halo = halo_ref[...].reshape(tokens, D)
    own_weight = dot_tn(own, own_back[...])
    halo_weight = dot_tn(halo, halo_back[...])
    weight_ref[0] = own_weight[:, :D]
    weight_ref[1] = own_weight[:, D : 2 * D] + halo_weight[:, :D]
    weight_ref[2] = own_weight[:, 2 * D :] + halo_weight[:, D:]


def self_back(
    group, scal, features, halo, qkv, halo_kv, mix, mid_grad, term_low, term_high,
    self_project, self_merge, norm_gains,
):
    rows, cols, _ = halo.shape
    tokens = rows * cols
    return pl.pallas_call(
        functools.partial(self_back_kernel, valid_slot=1 + group),
        grid=(1,),
        in_specs=[
            pl.BlockSpec(memory_space=pltpu.SMEM),
            pl.BlockSpec((rows, cols, D), lambda i: (group, 0, 0)),
            full_spec(halo.shape), full_spec(qkv.shape), full_spec(halo_kv.shape),
            full_spec(mix.shape),
            pl.BlockSpec((tokens, D), lambda i: (group, 0)),
            full_spec(term_low.shape), full_spec(term_high.shape),
            full_spec(self_project.shape), full_spec(self_merge.shape),
            full_spec(norm_gains.shape),
        ],
        out_specs=[
            full_spec((tokens, D)), full_spec((tokens, D)), full_spec((3, D, D)),
            full_spec((D, D)), full_spec((8, D)),
        ],
        out_shape=[
            jax.ShapeDtypeStruct((tokens, D), F32),
            jax.ShapeDtypeStruct((tokens, D), BF16),
            jax.ShapeDtypeStruct((3, D, D), F32),
            jax.ShapeDtypeStruct((D, D), F32),
            jax.ShapeDtypeStruct((8, D), F32),
        ],
        scratch_shapes=[
            pltpu.VMEM((rows, cols, D), BF16),
            pltpu.VMEM((rows, cols, 3 * D), BF16),
            pltpu.VMEM((rows, cols, 2 * D), BF16),
            pltpu.VMEM((tokens, 3 * D), BF16),
            pltpu.VMEM((tokens, 2 * D), BF16),
        ],
        name="self_back",
    )(scal, features, halo, qkv, halo_kv, mix, mid_grad, term_low, term_high,
      self_project, self_merge, norm_gains)


def scattered_sum(pieces, axis):
    count = lax.axis_size(axis)
    place = lax.axis_index(axis)
    current = pieces
    bit = 1
    while bit < count:
        pairs = current.reshape((current.shape[0] // 2, 2) + current.shape[1:])
        odd = (place & bit) != 0
        kept = jnp.where(odd, pairs[:, 1], pairs[:, 0])
        sent = jnp.where(odd, pairs[:, 0], pairs[:, 1]).astype(BF16)
        got = lax.ppermute(sent, axis, [(i, i ^ bit) for i in range(count)])
        current = kept + got.astype(F32)
        bit *= 2
    return current[0]


def body(
    features, window_offsets, self_project, self_merge, cross_project, cross_merge,
    feed_in, feed_out, norm_gains, result_grad,
):
    tile_rows, tile_cols = features.shape[0], features.shape[1]
    half_rows = tile_rows // 2
    tile_tokens = tile_rows * tile_cols
    half_tokens = tile_tokens // 2
    count = lax.axis_size("tiles")
    half_tiles = count // 2
    shift = count // 4
    position = lax.axis_index("tiles")
    image_place = (position + count - shift) % count
    offset = window_offsets[image_place // half_tiles]
    grad_scale = 1.0 / math.sqrt(count * tile_tokens)
    upper_valid = image_place % half_tiles != 0
    lower_valid = image_place % half_tiles != half_tiles - 1
    scal = jnp.stack(
        [offset, upper_valid.astype(jnp.int32), lower_valid.astype(jnp.int32)]
    )
    inner = [
        ((i + shift) % count, (i + 1 + shift) % count)
        for i in range(count)
        if i % half_tiles != half_tiles - 1
    ]
    to_next = inner
    to_previous = [(b, a) for a, b in inner]
    to_partner = [(i, (i + half_tiles) % count) for i in range(count)]

    halos = (
        lax.ppermute(features[half_rows:], "tiles", to_next),
        lax.ppermute(features[:half_rows], "tiles", to_previous),
    )
    parts = [
        self_forward(g, scal, features, halos[g], self_project, self_merge, norm_gains)
        for g in range(2)
    ]
    partners = [lax.ppermute(parts[g][0], "tiles", to_partner) for g in range(2)]
    middles = jnp.concatenate([parts[0][0], parts[1][0]], axis=0)

    block = min(512, half_tokens)
    upstream = result_grad.reshape(tile_tokens, D)
    q, kv_a, open_mix, open_stat = cross_open(block, middles, partners[0], cross_project)
    (kv_b, result, mid_grad, mix_grad, stats, grad_in, grad_out, grad_merge, gain_grad) = (
        cross_close(
            block, middles, partners[1], cross_project, q, open_mix, open_stat,
            cross_merge, feed_in, feed_out, norm_gains, upstream,
        )
    )
    half = half_tokens // 2
    carried, got = None, []
    for c in range(4):
        term, q_grad, cross_weight = cross_back(
            half, c % 2, block, q, mix_grad, stats, (kv_a, kv_b)[c // 2],
            partners[c // 2], cross_project,
            carried=carried, finish=(mid_grad, middles) if c == 3 else None,
        )
        carried = (q_grad, cross_weight)
        got.append(lax.ppermute(term, "tiles", to_partner))
    mid_grad = q_grad
    backs, terms = [], []
    for g in range(2):
        backs.append(
            self_back(
                g, scal, features, halos[g], parts[g][2], parts[g][3], parts[g][1],
                mid_grad, got[2 * g], got[2 * g + 1], self_project, self_merge, norm_gains,
            )
        )
        terms.append(
            lax.ppermute(backs[g][1], "tiles", (to_previous, to_next)[g])
        )
    from_next, from_previous = terms
    features_grad = jnp.concatenate(
        [
            backs[0][0] + from_previous.astype(F32),
            backs[1][0] + from_next.astype(F32),
        ],
        axis=0,
    ).reshape(tile_rows, tile_cols, D)

    self_weight = backs[0][2] + backs[1][2]
    merge_weight = backs[0][3] + backs[1][3]
    gains = jnp.concatenate(
        [backs[0][4][0:1] + backs[1][4][0:1], gain_grad[1:8]], axis=0
    )

    def cut(array):
        return array.reshape(count, array.shape[0] // count, D)

    summed = scattered_sum(
        jnp.concatenate(
            [cut(self_weight[b]) for b in range(3)]
            + [cut(merge_weight)]
            + [cut(cross_weight[b]) for b in range(3)]
            + [cut(grad_merge)]
            + [cut(grad_in[b]) for b in range(grad_in.shape[0])]
            + [cut(grad_out)]
            + [jnp.broadcast_to(gains[None], (count,) + gains.shape)],
            axis=1,
        ),
        "tiles",
    ) * grad_scale
    place = 0

    def take(rows, blocks):
        nonlocal place
        found = [summed[place + b * rows : place + (b + 1) * rows] for b in range(blocks)]
        place += rows * blocks
        return jnp.concatenate(found, axis=1)

    out_self = take(D // count, 3)
    out_self_merge = take(D // count, 1)
    out_cross = take(D // count, 3)
    out_cross_merge = take(D // count, 1)
    out_in = take(2 * D // count, feed_in.shape[1] // D)
    out_out = take(feed_out.shape[0] // count, 1)
    lanes = D // count
    out_gains = lax.dynamic_slice(summed[place : place + 3], (0, position * lanes), (3, lanes))
    return (
        result.reshape(tile_rows, tile_cols, D),
        features_grad,
        out_self,
        out_self_merge,
        out_cross,
        out_cross_merge,
        out_in,
        out_out,
        out_gains,
    )


def solution(mesh):
    whole = P(("groups", "tiles"), None, None)
    rows = P(("groups", "tiles"), None)
    return jax.shard_map(
        body,
        mesh=mesh,
        in_specs=(whole, P("groups"), P(), P(), P(), P(), P(), P(), P(), whole),
        out_specs=(whole, whole, rows, rows, rows, rows, rows, rows, P("groups", "tiles")),
        check_vma=False,
    )
```

```python
import functools
import math

import jax
import jax.numpy as jnp
from jax import lax
from jax.experimental import pallas as pl
from jax.experimental.pallas import tpu as pltpu
from jax.sharding import PartitionSpec as P


D = 128
WIN = 32

NORM_EPS = 1e-05
MASK_FILL = -1000000000.0
HALF_ROOT = 0.7071067811865476
DENSITY_COEF = 0.3989422804014327
LOG2_E = 1.4426950408889634
SCALE = D ** (-0.5)


LOCAL_LIMIT = pltpu.CompilerParams(vmem_limit_bytes=20 * 2**20)

F32 = jnp.float32
BF16 = jnp.bfloat16


def on_chip(array):
    return pltpu.with_memory_space_constraint(array, pltpu.VMEM)


def off_chip(array):
    return pltpu.with_memory_space_constraint(array, pltpu.HBM)


def dot_nn(a, b):
    return lax.dot_general(a, b, (((1,), (0,)), ((), ())), preferred_element_type=F32)


def dot_nt(a, b):
    return lax.dot_general(a, b, (((1,), (1,)), ((), ())), preferred_element_type=F32)


def dot_tn(a, b):
    return lax.dot_general(a, b, (((0,), (0,)), ((), ())), preferred_element_type=F32)


def layer_norm(values, gain):
    center = values - jnp.mean(values, axis=-1, keepdims=True)
    inverse = lax.rsqrt(jnp.mean(center * center, axis=-1, keepdims=True) + NORM_EPS)
    unit = center * inverse
    return unit * gain, unit, inverse


def norm_backward(upstream, gain, unit, inverse):
    scaled = upstream * gain
    grad = inverse * (
        scaled
        - jnp.mean(scaled, axis=-1, keepdims=True)
        - unit * jnp.mean(scaled * unit, axis=-1, keepdims=True)
    )
    return grad, jnp.sum(upstream * unit, axis=0, keepdims=True)


def roll_matrices(offset, size):
    i = lax.broadcasted_iota(jnp.int32, (size, size), 0)
    j = lax.broadcasted_iota(jnp.int32, (size, size), 1)
    row_source = i + offset
    row_source = jnp.where(row_source >= size, row_source - size, row_source)
    col_source = j + offset
    col_source = jnp.where(col_source >= size, col_source - size, col_source)
    forward = jnp.where(j == row_source, 1.0, 0.0).astype(BF16)
    back = jnp.where(i == col_source, 1.0, 0.0).astype(BF16)
    return forward, back


def pick(ref, cols, lanes):
    block = ref[:, cols, lanes]
    return block.reshape(block.shape[0] * block.shape[1], block.shape[2])


def self_forward_kernel(
    scal_ref, own_ref, halo_ref, project_ref, merge_ref, gains_ref,
    middle_ref, mix_ref, qkv_ref, halo_kv_ref, own_rolled, halo_rolled, mix_rolled,
    *, valid_slot,
):
    rows, cols = own_ref.shape[0], own_ref.shape[1]
    forward, back = roll_matrices(scal_ref[0], cols)
    valid = scal_ref[valid_slot] > 0
    for r in range(rows):
        own_rolled[r] = dot_nn(forward, own_ref[r]).astype(BF16)
        halo_rolled[r] = dot_nn(forward, halo_ref[r]).astype(BF16)
    tokens = rows * cols
    qkv_ref[...] = (
        dot_nn(own_rolled[...].reshape(tokens, D), project_ref[...])
        .astype(BF16).reshape(rows, cols, 3 * D)
    )
    halo_kv_ref[...] = (
        dot_nn(halo_rolled[...].reshape(tokens, D), project_ref[:, D:])
        .astype(BF16).reshape(rows, cols, 2 * D)
    )
    for w in range(cols // WIN):
        span = slice(w * WIN, (w + 1) * WIN)
        q = pick(qkv_ref, span, slice(0, D))
        s_own = dot_nt(q, pick(qkv_ref, span, slice(D, 2 * D))) * SCALE
        s_halo = dot_nt(q, pick(halo_kv_ref, span, slice(0, D))) * SCALE
        s_halo = jnp.where(valid, s_halo, MASK_FILL)
        top = jnp.maximum(
            jnp.max(s_own, axis=-1, keepdims=True), jnp.max(s_halo, axis=-1, keepdims=True)
        )
        p_own = jnp.exp(s_own - top)
        p_halo = jnp.exp(s_halo - top)
        inv = 1.0 / (
            jnp.sum(p_own, axis=-1, keepdims=True) + jnp.sum(p_halo, axis=-1, keepdims=True)
        )
        mixed = dot_nn(
            (p_own * inv).astype(BF16), pick(qkv_ref, span, slice(2 * D, 3 * D))
        ) + dot_nn((p_halo * inv).astype(BF16), pick(halo_kv_ref, span, slice(D, 2 * D)))
        mix_rolled[:, span, :] = mixed.astype(BF16).reshape(rows, WIN, D)
    for r in range(rows):
        mix_ref[r * cols : (r + 1) * cols, :] = dot_nn(back, mix_rolled[r]).astype(BF16)
    normed, _, _ = layer_norm(dot_nn(mix_ref[...], merge_ref[...]), gains_ref[0:1, :])
    middle_ref[...] = (own_ref[...].reshape(tokens, D).astype(F32) + normed).astype(BF16)


def full_spec(shape):
    zeros = (0,) * len(shape)
    return pl.BlockSpec(shape, lambda *_: zeros)


def self_forward(group, scal, features, halo, self_project, self_merge, norm_gains):
    rows, cols, _ = halo.shape
    tokens = rows * cols
    return pl.pallas_call(
        functools.partial(self_forward_kernel, valid_slot=1 + group),
        grid=(1,),
        in_specs=[
            pl.BlockSpec(memory_space=pltpu.SMEM),
            pl.BlockSpec((rows, cols, D), lambda i: (group, 0, 0)),
            full_spec(halo.shape),
            full_spec(self_project.shape),
            full_spec(self_merge.shape),
            full_spec(norm_gains.shape),
        ],
        out_specs=[
            full_spec((tokens, D)),
            full_spec((tokens, D)),
            full_spec((rows, cols, 3 * D)),
            full_spec((rows, cols, 2 * D)),
        ],
        out_shape=[
            jax.ShapeDtypeStruct((tokens, D), BF16),
            pltpu.VMEM((tokens, D), BF16),
            pltpu.VMEM((rows, cols, 3 * D), BF16),
            pltpu.VMEM((rows, cols, 2 * D), BF16),
        ],
        scratch_shapes=[pltpu.VMEM((rows, cols, D), BF16)] * 3,
        compiler_params=LOCAL_LIMIT,
        name="self_forward",
    )(scal, features, halo, self_project, self_merge, norm_gains)


def cross_open_kernel(middle_ref, partner_ref, project_ref, q_ref, kv_ref, mix_ref, stat_ref):
    @pl.when(pl.program_id(0) == 0)
    def _():
        kv_ref[...] = dot_nn(partner_ref[...], project_ref[:, D:]).astype(BF16)

    q = dot_nn(middle_ref[...], project_ref[:, :D]).astype(BF16)
    q_ref[...] = q
    logits = dot_nt(q, kv_ref[:, :D]) * (SCALE * LOG2_E)
    top = jnp.max(logits, axis=-1, keepdims=True)
    raised = jnp.exp2(logits - top)
    total = jnp.sum(raised, axis=-1, keepdims=True)
    mix_ref[...] = dot_nn(raised.astype(BF16), kv_ref[:, D:])
    lane = lax.broadcasted_iota(jnp.int32, stat_ref.shape, 1)
    stat_ref[...] = jnp.where(lane == 0, top, total)


def cross_open(block, middles, partner, cross_project):
    chunk = partner.shape[0]
    tokens = middles.shape[0]
    row = lambda i: (i, 0)
    return pl.pallas_call(
        cross_open_kernel,
        grid=(tokens // block,),
        in_specs=[
            pl.BlockSpec((block, D), row),
            full_spec(partner.shape),
            full_spec(cross_project.shape),
        ],
        out_specs=[
            pl.BlockSpec((block, D), row),
            full_spec((chunk, 2 * D)),
            pl.BlockSpec((block, D), row),
            pl.BlockSpec((block, D), row),
        ],
        out_shape=[
            jax.ShapeDtypeStruct((tokens, D), BF16),
            jax.ShapeDtypeStruct((chunk, 2 * D), BF16),
            jax.ShapeDtypeStruct((tokens, D), F32),
            jax.ShapeDtypeStruct((tokens, D), F32),
        ],
        compiler_params=LOCAL_LIMIT,
        name="cross_open",
    )(middles, partner, cross_project)


def cross_close_kernel(
    middle_ref, partner_ref, project_ref, q_ref, open_mix_ref, open_stat_ref,
    merge_ref, feed_in_ref, feed_out_ref, gains_ref, upstream_ref,
    kv_ref, result_ref, mid_grad_ref, mix_grad_ref, stat_ref,
    grad_in_ref, grad_out_ref, grad_merge_ref, grad_gain_ref,
):
    @pl.when(pl.program_id(0) == 0)
    def _():
        kv_ref[...] = dot_nn(partner_ref[...], project_ref[:, D:]).astype(BF16)
        grad_in_ref[...] = jnp.zeros_like(grad_in_ref)
        grad_out_ref[...] = jnp.zeros_like(grad_out_ref)
        grad_merge_ref[...] = jnp.zeros_like(grad_merge_ref)
        grad_gain_ref[...] = jnp.zeros_like(grad_gain_ref)

    block = middle_ref.shape[0]
    logits = dot_nt(q_ref[...], kv_ref[:, :D]) * (SCALE * LOG2_E)
    open_top = open_stat_ref[:, 0:1]
    open_total = open_stat_ref[:, 1:2]
    top = jnp.maximum(jnp.max(logits, axis=-1, keepdims=True), open_top)
    raised = jnp.exp2(logits - top)
    carry = jnp.exp2(open_top - top)
    total = jnp.sum(raised, axis=-1, keepdims=True) + open_total * carry
    mixed = dot_nn(raised.astype(BF16), kv_ref[:, D:]) + open_mix_ref[...] * carry
    mixed = mixed * (1.0 / total)
    log_total = top + jnp.log2(total)
    cross_mix = mixed.astype(BF16)

    middle = middle_ref[...]
    gain_cross = gains_ref[1:2, :]
    gain_feed = gains_ref[2:3, :]
    cross_full, cross_unit, cross_inverse = layer_norm(
        dot_nn(cross_mix, merge_ref[...]), gain_cross
    )
    cross_normed = cross_full.astype(BF16)
    feed_pre = dot_nn(middle, feed_in_ref[:D, :]) + dot_nn(cross_normed, feed_in_ref[D:, :])
    bell = 0.5 * (1.0 + lax.erf(feed_pre * HALF_ROOT))
    hidden = (feed_pre * bell).astype(BF16)
    slope = bell + feed_pre * (jnp.exp(-0.5 * feed_pre * feed_pre) * DENSITY_COEF)
    feed_normed, feed_unit, feed_inverse = layer_norm(
        dot_nn(hidden, feed_out_ref[...]), gain_feed
    )
    result_ref[...] = (middle.astype(F32) + feed_normed).astype(BF16)
    upstream = upstream_ref[...]
    post_full, gain_grad_feed = norm_backward(upstream, gain_feed, feed_unit, feed_inverse)
    grad_post = post_full.astype(BF16)
    grad_pre = (dot_nt(grad_post, feed_out_ref[...]) * slope).astype(BF16)
    grad_joined = dot_nt(grad_pre, feed_in_ref[...])
    mid_grad_ref[...] = upstream + grad_joined[:, :D]
    lanes = grad_in_ref.shape[0]
    grad_low = dot_tn(middle, grad_pre)
    grad_high = dot_tn(cross_normed, grad_pre)
    for b in range(lanes):
        grad_in_ref[b, :D, :] += grad_low[:, b * D : (b + 1) * D]
        grad_in_ref[b, D:, :] += grad_high[:, b * D : (b + 1) * D]
    grad_out_ref[...] += dot_tn(hidden, grad_post)
    merged_full, gain_grad_cross = norm_backward(
        grad_joined[:, D:], gain_cross, cross_unit, cross_inverse
    )
    grad_merged = merged_full.astype(BF16)
    grad_merge_ref[...] += dot_tn(cross_mix, grad_merged)
    mix_grad = dot_nt(grad_merged, merge_ref[...]).astype(BF16)
    mix_grad_ref[...] = mix_grad
    inner = jnp.sum(mix_grad.astype(F32) * mixed, axis=-1, keepdims=True)
    lane = lax.broadcasted_iota(jnp.int32, (block, D), 1)
    stats = jnp.where(lane == 0, log_total, inner)
    stat_ref[...] = stats.T[: stat_ref.shape[0], :]
    grad_gain_ref[1:2, :] += gain_grad_cross
    grad_gain_ref[2:3, :] += gain_grad_feed


def cross_close(
    block, middles, partner, cross_project, q, open_mix, open_stat,
    cross_merge, feed_in, feed_out, norm_gains, upstream,
):
    tokens = middles.shape[0]
    chunk = partner.shape[0]
    hidden = feed_in.shape[1]
    row = lambda i: (i, 0)
    tile = pl.BlockSpec((block, D), row)
    return pl.pallas_call(
        cross_close_kernel,
        grid=(tokens // block,),
        in_specs=[
            tile, full_spec(partner.shape), full_spec(cross_project.shape), tile, tile, tile,
            full_spec(cross_merge.shape), full_spec(feed_in.shape), full_spec(feed_out.shape),
            full_spec(norm_gains.shape), tile,
        ],
        out_specs=[
            full_spec((chunk, 2 * D)), tile, tile, tile,
            pl.BlockSpec((8, block), lambda i: (0, i)),
            full_spec((hidden // D, 2 * D, D)), full_spec((hidden, D)), full_spec((D, D)),
            full_spec((8, D)),
        ],
        out_shape=[
            jax.ShapeDtypeStruct((chunk, 2 * D), BF16),
            jax.ShapeDtypeStruct((tokens, D), BF16),
            jax.ShapeDtypeStruct((tokens, D), F32),
            jax.ShapeDtypeStruct((tokens, D), BF16),
            jax.ShapeDtypeStruct((8, tokens), F32),
            jax.ShapeDtypeStruct((hidden // D, 2 * D, D), F32),
            jax.ShapeDtypeStruct((hidden, D), F32),
            jax.ShapeDtypeStruct((D, D), F32),
            jax.ShapeDtypeStruct((8, D), F32),
        ],
        compiler_params=LOCAL_LIMIT,
        name="cross_close",
    )(middles, partner, cross_project, q, open_mix, open_stat,
      cross_merge, feed_in, feed_out, norm_gains, upstream)


def cross_back_kernel(*refs, first, last, q_block):
    refs = list(refs)
    q_ref, grad_ref, stat_ref, kv_ref, partner_ref, project_ref = refs[:6]
    refs = refs[6:]
    if not first:
        q_in_ref, weight_in_ref = refs[:2]
        refs = refs[2:]
    if last:
        mid_grad_ref, middle_ref = refs[:2]
        refs = refs[2:]
    term_ref, q_out_ref, weight_ref, k_acc, v_acc, q_acc = refs
    step = pl.program_id(0)

    @pl.when(step == 0)
    def _():
        if first:
            q_acc[...] = jnp.zeros_like(q_acc)
            weight_ref[...] = jnp.zeros_like(weight_ref)
        else:
            q_acc[...] = q_in_ref[...]
            weight_ref[...] = weight_in_ref[...]

    k_acc[...] = jnp.zeros_like(k_acc)
    v_acc[...] = jnp.zeros_like(v_acc)
    keys = kv_ref[:, :D]
    values = kv_ref[:, D:]
    tokens = q_ref.shape[0]

    @pl.loop(0, tokens // q_block)
    def _(j):
        span = pl.ds(pl.multiple_of(j * q_block, q_block), q_block)
        q = q_ref[span, :]
        grad = grad_ref[span, :]
        log_total = stat_ref[0:1, span]
        inner = stat_ref[1:2, span]
        shares = jnp.exp2(dot_nt(keys, q) * (SCALE * LOG2_E) - log_total)
        slopes = dot_nt(values, grad) - inner
        v_acc[...] += dot_nn(shares.astype(BF16), grad)
        logit_grad = (shares * slopes).astype(BF16)
        k_acc[...] += dot_nn(logit_grad, q)
        q_acc[span, :] += dot_tn(logit_grad, keys)

    pair = jnp.concatenate(
        [(k_acc[...] * SCALE).astype(BF16), v_acc[...].astype(BF16)], axis=1
    )
    term_ref[...] = dot_nt(pair, project_ref[:, D:]).astype(BF16)
    pair_weight = dot_tn(partner_ref[...], pair)
    weight_ref[1] += pair_weight[:, :D]
    weight_ref[2] += pair_weight[:, D:]

    @pl.when(step == pl.num_programs(0) - 1)
    def _():
        if last:
            q_grad = (q_acc[...] * SCALE).astype(BF16)
            q_out_ref[...] = mid_grad_ref[...] + dot_nt(q_grad, project_ref[:, :D])
            weight_ref[0] += dot_tn(middle_ref[...], q_grad)
        else:
            q_out_ref[...] = q_acc[...]


def cross_back(
    block, index, q_block, q, mix_grad, stats, kv, partner, cross_project,
    carried=None, finish=None,
):
    tokens = q.shape[0]
    first, last = carried is None, finish is not None
    args = [q, mix_grad, stats, kv, partner, cross_project]
    specs = [
        full_spec(q.shape), full_spec(mix_grad.shape), full_spec(stats.shape),
        pl.BlockSpec((block, 2 * D), lambda i: (index, 0)),
        pl.BlockSpec((block, D), lambda i: (index, 0)),
        full_spec(cross_project.shape),
    ]
    for extra in (carried or ()) + (finish or ()):
        args.append(extra)
        specs.append(full_spec(extra.shape))
    return pl.pallas_call(
        functools.partial(cross_back_kernel, first=first, last=last, q_block=q_block),
        grid=(1,),
        in_specs=specs,
        out_specs=[
            full_spec((block, D)), full_spec((tokens, D)), full_spec((3, D, D)),
        ],
        out_shape=[
            jax.ShapeDtypeStruct((block, D), BF16),
            jax.ShapeDtypeStruct((tokens, D), F32),
            jax.ShapeDtypeStruct((3, D, D), F32),
        ],
        scratch_shapes=[
            pltpu.VMEM((block, D), F32), pltpu.VMEM((block, D), F32), pltpu.VMEM((tokens, D), F32)
        ],
        compiler_params=LOCAL_LIMIT,
        name="cross_back",
    )(*args)


def self_back_kernel(
    scal_ref, own_ref, halo_ref, qkv_ref, halo_kv_ref, mix_ref, mid_grad_ref,
    term_low_ref, term_high_ref, project_ref, merge_ref, gains_ref,
    feature_grad_ref, halo_term_ref, weight_ref, merge_grad_ref, gain_ref,
    mix_grad, own_grad, halo_grad, own_back, halo_back,
    *, valid_slot,
):
    rows, cols = own_ref.shape[0], own_ref.shape[1]
    tokens = rows * cols
    forward, back = roll_matrices(scal_ref[0], cols)
    valid = scal_ref[valid_slot] > 0
    upstream = mid_grad_ref[...] + jnp.concatenate(
        [term_low_ref[...].astype(F32), term_high_ref[...].astype(F32)], axis=0
    )
    gain = gains_ref[0:1, :]
    _, unit, inverse = layer_norm(dot_nn(mix_ref[...], merge_ref[...]), gain)
    merged_full, gain_grad = norm_backward(upstream, gain, unit, inverse)
    gain_ref[...] = jnp.broadcast_to(gain_grad, gain_ref.shape)
    grad_merged = merged_full.astype(BF16)
    merge_grad_ref[...] = dot_tn(mix_ref[...], grad_merged)
    plain_grad = dot_nt(grad_merged, merge_ref[...]).astype(BF16)
    for r in range(rows):
        mix_grad[r] = dot_nn(forward, plain_grad[r * cols : (r + 1) * cols, :]).astype(BF16)
    for w in range(cols // WIN):
        span = slice(w * WIN, (w + 1) * WIN)
        q = pick(qkv_ref, span, slice(0, D))
        k_own = pick(qkv_ref, span, slice(D, 2 * D))
        k_halo = pick(halo_kv_ref, span, slice(0, D))
        grad = pick(mix_grad, span, slice(0, D))
        s_own = dot_nt(k_own, q) * SCALE
        s_halo = jnp.where(valid, dot_nt(k_halo, q) * SCALE, MASK_FILL)
        top = jnp.maximum(
            jnp.max(s_own, axis=0, keepdims=True), jnp.max(s_halo, axis=0, keepdims=True)
        )
        p_own = jnp.exp(s_own - top)
        p_halo = jnp.exp(s_halo - top)
        inv = 1.0 / (
            jnp.sum(p_own, axis=0, keepdims=True) + jnp.sum(p_halo, axis=0, keepdims=True)
        )
        p_own = p_own * inv
        p_halo = p_halo * inv
        d_own = dot_nt(pick(qkv_ref, span, slice(2 * D, 3 * D)), grad)
        d_halo = dot_nt(pick(halo_kv_ref, span, slice(D, 2 * D)), grad)
        inner = jnp.sum(p_own * d_own, axis=0, keepdims=True) + jnp.sum(
            p_halo * d_halo, axis=0, keepdims=True
        )
        l_own = (p_own * (d_own - inner) * SCALE).astype(BF16)
        l_halo = (p_halo * (d_halo - inner) * SCALE).astype(BF16)
        q_grad = dot_tn(l_own, k_own) + dot_tn(l_halo, k_halo)
        shape = (rows, WIN, D)
        own_grad[:, span, :D] = q_grad.astype(BF16).reshape(shape)
        own_grad[:, span, D : 2 * D] = dot_nn(l_own, q).astype(BF16).reshape(shape)
        own_grad[:, span, 2 * D :] = dot_nn(p_own.astype(BF16), grad).astype(BF16).reshape(shape)
        halo_grad[:, span, :D] = dot_nn(l_halo, q).astype(BF16).reshape(shape)
        halo_grad[:, span, D:] = dot_nn(p_halo.astype(BF16), grad).astype(BF16).reshape(shape)
    for r in range(rows):
        line = slice(r * cols, (r + 1) * cols)
        halo_back[line, :] = dot_nn(back, halo_grad[r]).astype(BF16)
        own_back[line, :] = dot_nn(back, own_grad[r]).astype(BF16)
    halo_term_ref[...] = dot_nt(halo_back[...], project_ref[:, D:]).astype(BF16)
    feature_grad_ref[...] = upstream + dot_nt(own_back[...], project_ref[...])
    own = own_ref[...].reshape(tokens, D)
    halo = halo_ref[...].reshape(tokens, D)
    own_weight = dot_tn(own, own_back[...])
    halo_weight = dot_tn(halo, halo_back[...])
    weight_ref[0] = own_weight[:, :D]
    weight_ref[1] = own_weight[:, D : 2 * D] + halo_weight[:, :D]
    weight_ref[2] = own_weight[:, 2 * D :] + halo_weight[:, D:]


def self_back(
    group, scal, features, halo, qkv, halo_kv, mix, mid_grad, term_low, term_high,
    self_project, self_merge, norm_gains,
):
    rows, cols, _ = halo.shape
    tokens = rows * cols
    return pl.pallas_call(
        functools.partial(self_back_kernel, valid_slot=1 + group),
        grid=(1,),
        in_specs=[
            pl.BlockSpec(memory_space=pltpu.SMEM),
            pl.BlockSpec((rows, cols, D), lambda i: (group, 0, 0)),
            full_spec(halo.shape), full_spec(qkv.shape), full_spec(halo_kv.shape),
            full_spec(mix.shape),
            pl.BlockSpec((tokens, D), lambda i: (group, 0)),
            full_spec(term_low.shape), full_spec(term_high.shape),
            full_spec(self_project.shape), full_spec(self_merge.shape),
            full_spec(norm_gains.shape),
        ],
        out_specs=[
            full_spec((tokens, D)), full_spec((tokens, D)), full_spec((3, D, D)),
            full_spec((D, D)), full_spec((8, D)),
        ],
        out_shape=[
            jax.ShapeDtypeStruct((tokens, D), F32),
            jax.ShapeDtypeStruct((tokens, D), BF16),
            jax.ShapeDtypeStruct((3, D, D), F32),
            jax.ShapeDtypeStruct((D, D), F32),
            jax.ShapeDtypeStruct((8, D), F32),
        ],
        scratch_shapes=[
            pltpu.VMEM((rows, cols, D), BF16),
            pltpu.VMEM((rows, cols, 3 * D), BF16),
            pltpu.VMEM((rows, cols, 2 * D), BF16),
            pltpu.VMEM((tokens, 3 * D), BF16),
            pltpu.VMEM((tokens, 2 * D), BF16),
        ],
        compiler_params=LOCAL_LIMIT,
        name="self_back",
    )(scal, features, halo, qkv, halo_kv, mix, mid_grad, term_low, term_high,
      self_project, self_merge, norm_gains)


def scattered_sum(pieces, axis):
    count = lax.axis_size(axis)
    place = lax.axis_index(axis)
    current = pieces
    bit = 1
    while bit < count:
        pairs = current.reshape((current.shape[0] // 2, 2) + current.shape[1:])
        odd = (place & bit) != 0
        kept = jnp.where(odd, pairs[:, 1], pairs[:, 0])
        sent = jnp.where(odd, pairs[:, 0], pairs[:, 1]).astype(BF16)
        got = lax.ppermute(sent, axis, [(i, i ^ bit) for i in range(count)])
        current = kept + got.astype(F32)
        bit *= 2
    return current[0]


def body(
    features, window_offsets, self_project, self_merge, cross_project, cross_merge,
    feed_in, feed_out, norm_gains, result_grad,
):
    tile_rows, tile_cols = features.shape[0], features.shape[1]
    half_rows = tile_rows // 2
    tile_tokens = tile_rows * tile_cols
    half_tokens = tile_tokens // 2
    count = lax.axis_size("tiles")
    half_tiles = count // 2
    shift = count // 4
    position = lax.axis_index("tiles")
    image_place = (position + count - shift) % count
    offset = window_offsets[image_place // half_tiles]
    grad_scale = 1.0 / math.sqrt(count * tile_tokens)
    upper_valid = image_place % half_tiles != 0
    lower_valid = image_place % half_tiles != half_tiles - 1
    scal = jnp.stack(
        [offset, upper_valid.astype(jnp.int32), lower_valid.astype(jnp.int32)]
    )
    inner = [
        ((i + shift) % count, (i + 1 + shift) % count)
        for i in range(count)
        if i % half_tiles != half_tiles - 1
    ]
    to_next = inner
    to_previous = [(b, a) for a, b in inner]
    to_partner = [(i, (i + half_tiles) % count) for i in range(count)]

    raw_features = features
    features = off_chip(features)
    self_project, self_merge, cross_project, cross_merge, feed_in, feed_out, norm_gains = (
        off_chip(w)
        for w in (
            self_project, self_merge, cross_project, cross_merge, feed_in, feed_out, norm_gains
        )
    )
    halos = (
        lax.ppermute(raw_features[half_rows:], "tiles", to_next),
        lax.ppermute(raw_features[:half_rows], "tiles", to_previous),
    )
    parts = [
        self_forward(g, scal, features, halos[g], self_project, self_merge, norm_gains)
        for g in range(2)
    ]
    partners = [lax.ppermute(parts[g][0], "tiles", to_partner) for g in range(2)]
    middles = jnp.concatenate([parts[0][0], parts[1][0]], axis=0)

    block = min(512, half_tokens)
    upstream = off_chip(result_grad.reshape(tile_tokens, D))
    q, kv_a, open_mix, open_stat = cross_open(block, middles, partners[0], cross_project)
    (kv_b, result, mid_grad, mix_grad, stats, grad_in, grad_out, grad_merge, gain_grad) = (
        cross_close(
            block, middles, partners[1], cross_project, q, open_mix, open_stat,
            cross_merge, feed_in, feed_out, norm_gains, upstream,
        )
    )
    half = half_tokens // 2
    carried, got = None, []
    for c in range(4):
        term, q_grad, cross_weight = cross_back(
            half, c % 2, block, q, mix_grad, stats, (kv_a, kv_b)[c // 2],
            partners[c // 2], cross_project,
            carried=carried, finish=(mid_grad, middles) if c == 3 else None,
        )
        carried = (q_grad, cross_weight)
        got.append(lax.ppermute(term, "tiles", to_partner))
    mid_grad = q_grad
    backs, terms = [], []
    for g in range(2):
        backs.append(
            self_back(
                g, scal, features, halos[g],
                on_chip(parts[g][2]), on_chip(parts[g][3]), on_chip(parts[g][1]),
                mid_grad, got[2 * g], got[2 * g + 1], self_project, self_merge, norm_gains,
            )
        )
        terms.append(
            lax.ppermute(backs[g][1], "tiles", (to_previous, to_next)[g])
        )
    from_next, from_previous = terms
    features_grad = jnp.concatenate(
        [
            backs[0][0] + from_previous.astype(F32),
            backs[1][0] + from_next.astype(F32),
        ],
        axis=0,
    ).reshape(tile_rows, tile_cols, D)

    self_weight = backs[0][2] + backs[1][2]
    merge_weight = backs[0][3] + backs[1][3]
    gains = jnp.concatenate(
        [backs[0][4][0:1] + backs[1][4][0:1], gain_grad[1:8]], axis=0
    )

    def cut(array):
        return array.reshape(count, array.shape[0] // count, D)

    summed = scattered_sum(
        jnp.concatenate(
            [cut(self_weight[b]) for b in range(3)]
            + [cut(merge_weight)]
            + [cut(cross_weight[b]) for b in range(3)]
            + [cut(grad_merge)]
            + [cut(grad_in[b]) for b in range(grad_in.shape[0])]
            + [cut(grad_out)]
            + [jnp.broadcast_to(gains[None], (count,) + gains.shape)],
            axis=1,
        ),
        "tiles",
    ) * grad_scale
    place = 0

    def take(rows, blocks):
        nonlocal place
        found = [summed[place + b * rows : place + (b + 1) * rows] for b in range(blocks)]
        place += rows * blocks
        return jnp.concatenate(found, axis=1)

    out_self = take(D // count, 3)
    out_self_merge = take(D // count, 1)
    out_cross = take(D // count, 3)
    out_cross_merge = take(D // count, 1)
    out_in = take(2 * D // count, feed_in.shape[1] // D)
    out_out = take(feed_out.shape[0] // count, 1)
    lanes = D // count
    out_gains = lax.dynamic_slice(summed[place : place + 3], (0, position * lanes), (3, lanes))
    return (
        result.reshape(tile_rows, tile_cols, D),
        features_grad,
        out_self,
        out_self_merge,
        out_cross,
        out_cross_merge,
        out_in,
        out_out,
        out_gains,
    )


def solution(mesh):
    whole = P(("groups", "tiles"), None, None)
    rows = P(("groups", "tiles"), None)
    return jax.shard_map(
        body,
        mesh=mesh,
        in_specs=(whole, P("groups"), P(), P(), P(), P(), P(), P(), P(), whole),
        out_specs=(whole, whole, rows, rows, rows, rows, rows, rows, P("groups", "tiles")),
        check_vma=False,
    )
```

```python
import functools
import math

import jax
import jax.numpy as jnp
from jax import lax
from jax.experimental import pallas as pl
from jax.experimental.pallas import tpu as pltpu
from jax.sharding import PartitionSpec as P


D = 128
WIN = 32

NORM_EPS = 1e-05
MASK_FILL = -1000000000.0
HALF_ROOT = 0.7071067811865476
DENSITY_COEF = 0.3989422804014327
LOG2_E = 1.4426950408889634
SCALE = D ** (-0.5)
PIECE = 256


LOCAL_LIMIT = pltpu.CompilerParams(vmem_limit_bytes=28 * 2**20)

F32 = jnp.float32
BF16 = jnp.bfloat16


def on_chip(array):
    return pltpu.with_memory_space_constraint(array, pltpu.VMEM)


def off_chip(array):
    return pltpu.with_memory_space_constraint(array, pltpu.HBM)


def dot_nn(a, b):
    return lax.dot_general(a, b, (((1,), (0,)), ((), ())), preferred_element_type=F32)


def dot_nt(a, b):
    return lax.dot_general(a, b, (((1,), (1,)), ((), ())), preferred_element_type=F32)


def dot_tn(a, b):
    return lax.dot_general(a, b, (((0,), (0,)), ((), ())), preferred_element_type=F32)


def layer_norm(values, gain):
    center = values - jnp.mean(values, axis=-1, keepdims=True)
    inverse = lax.rsqrt(jnp.mean(center * center, axis=-1, keepdims=True) + NORM_EPS)
    unit = center * inverse
    return unit * gain, unit, inverse


def norm_backward(upstream, gain, unit, inverse):
    scaled = upstream * gain
    grad = inverse * (
        scaled
        - jnp.mean(scaled, axis=-1, keepdims=True)
        - unit * jnp.mean(scaled * unit, axis=-1, keepdims=True)
    )
    return grad, jnp.sum(upstream * unit, axis=0, keepdims=True)


def roll_matrices(offset, size):
    i = lax.broadcasted_iota(jnp.int32, (size, size), 0)
    j = lax.broadcasted_iota(jnp.int32, (size, size), 1)
    row_source = i + offset
    row_source = jnp.where(row_source >= size, row_source - size, row_source)
    col_source = j + offset
    col_source = jnp.where(col_source >= size, col_source - size, col_source)
    forward = jnp.where(j == row_source, 1.0, 0.0).astype(BF16)
    back = jnp.where(i == col_source, 1.0, 0.0).astype(BF16)
    return forward, back


def whereabouts(offsets_ref, place_ref, count, group):
    half = count // 2
    image_place = lax.rem(place_ref[0] + (count - count // 4), count)
    inside = lax.rem(image_place, half) != (0, half - 1)[group]
    return offsets_ref[lax.div(image_place, half)], inside


def pick(ref, cols, lanes):
    block = ref[:, cols, lanes]
    return block.reshape(block.shape[0] * block.shape[1], block.shape[2])


def self_forward_kernel(
    offsets_ref, place_ref, own_ref, halo_ref, project_ref, merge_ref, gains_ref,
    middle_ref, mix_ref, qkv_ref, halo_kv_ref, own_rolled, halo_rolled, mix_rolled,
    *, count, group,
):
    rows, cols = own_ref.shape[0], own_ref.shape[1]
    offset, valid = whereabouts(offsets_ref, place_ref, count, group)
    forward, back = roll_matrices(offset, cols)
    for r in range(rows):
        own_rolled[r] = dot_nn(forward, own_ref[r]).astype(BF16)
        halo_rolled[r] = dot_nn(forward, halo_ref[r]).astype(BF16)
    tokens = rows * cols
    qkv_ref[...] = (
        dot_nn(own_rolled[...].reshape(tokens, D), project_ref[...])
        .astype(BF16).reshape(rows, cols, 3 * D)
    )
    halo_kv_ref[...] = (
        dot_nn(halo_rolled[...].reshape(tokens, D), project_ref[:, D:])
        .astype(BF16).reshape(rows, cols, 2 * D)
    )
    for w in range(cols // WIN):
        span = slice(w * WIN, (w + 1) * WIN)
        q = pick(qkv_ref, span, slice(0, D))
        s_own = dot_nt(q, pick(qkv_ref, span, slice(D, 2 * D))) * SCALE
        s_halo = dot_nt(q, pick(halo_kv_ref, span, slice(0, D))) * SCALE
        s_halo = jnp.where(valid, s_halo, MASK_FILL)
        top = jnp.maximum(
            jnp.max(s_own, axis=-1, keepdims=True), jnp.max(s_halo, axis=-1, keepdims=True)
        )
        p_own = jnp.exp(s_own - top)
        p_halo = jnp.exp(s_halo - top)
        inv = 1.0 / (
            jnp.sum(p_own, axis=-1, keepdims=True) + jnp.sum(p_halo, axis=-1, keepdims=True)
        )
        mixed = dot_nn(
            (p_own * inv).astype(BF16), pick(qkv_ref, span, slice(2 * D, 3 * D))
        ) + dot_nn((p_halo * inv).astype(BF16), pick(halo_kv_ref, span, slice(D, 2 * D)))
        mix_rolled[:, span, :] = mixed.astype(BF16).reshape(rows, WIN, D)
    for r in range(rows):
        mix_ref[r * cols : (r + 1) * cols, :] = dot_nn(back, mix_rolled[r]).astype(BF16)
    normed, _, _ = layer_norm(dot_nn(mix_ref[...], merge_ref[...]), gains_ref[0:1, :])
    middle_ref[...] = (own_ref[...].reshape(tokens, D).astype(F32) + normed).astype(BF16)


def full_spec(shape):
    zeros = (0,) * len(shape)
    return pl.BlockSpec(shape, lambda *_: zeros)


def self_forward(group, offsets, place, features, halo, self_project, self_merge, norm_gains):
    rows, cols, _ = halo.shape
    tokens = rows * cols
    return pl.pallas_call(
        functools.partial(
            self_forward_kernel, count=lax.axis_size("tiles"), group=group
        ),
        grid=(1,),
        in_specs=[
            pl.BlockSpec(memory_space=pltpu.SMEM),
            pl.BlockSpec(memory_space=pltpu.SMEM),
            pl.BlockSpec((rows, cols, D), lambda i: (group, 0, 0)),
            full_spec(halo.shape),
            full_spec(self_project.shape),
            full_spec(self_merge.shape),
            full_spec(norm_gains.shape),
        ],
        out_specs=[
            full_spec((tokens, D)),
            full_spec((tokens, D)),
            full_spec((rows, cols, 3 * D)),
            full_spec((rows, cols, 2 * D)),
        ],
        out_shape=[
            jax.ShapeDtypeStruct((tokens, D), BF16),
            pltpu.VMEM((tokens, D), BF16),
            pltpu.VMEM((rows, cols, 3 * D), BF16),
            pltpu.VMEM((rows, cols, 2 * D), BF16),
        ],
        scratch_shapes=[pltpu.VMEM((rows, cols, D), BF16)] * 3,
        compiler_params=LOCAL_LIMIT,
        name="self_forward",
    )(offsets, place, features, halo, self_project, self_merge, norm_gains)


def key_scores(kv_ref, q):
    return dot_nt(kv_ref[:, :D], q) * (SCALE * LOG2_E)


def cross_open_kernel(
    low_ref, high_ref, partner_ref, project_ref,
    middle_ref, q_ref, kv_ref, mix_ref, stat_ref, raised_ref, values_t,
):
    step = pl.program_id(0)
    block = low_ref.shape[0]

    @pl.when(step == 0)
    def _():
        kv_ref[...] = dot_nn(partner_ref[...], project_ref[:, D:]).astype(BF16)
        values_t[...] = kv_ref[:, D:].T

    middle = jnp.where(step < pl.num_programs(0) // 2, low_ref[...], high_ref[...])
    middle_ref[...] = middle
    q = dot_nn(middle, project_ref[:, :D]).astype(BF16)
    q_ref[...] = q
    base = pl.multiple_of(step * block, block)
    row = lax.broadcasted_iota(jnp.int32, (stat_ref.shape[0], PIECE), 0)
    logits = key_scores(kv_ref, q[:PIECE])
    for start in range(0, block, PIECE):
        span = slice(start, start + PIECE)
        current = logits
        if start + PIECE < block:
            logits = key_scores(kv_ref, q[start + PIECE : start + 2 * PIECE])
        top = jnp.max(current, axis=0, keepdims=True)
        raised = jnp.exp2(current - top)
        total = jnp.sum(raised, axis=0, keepdims=True)
        packed = raised.astype(BF16)
        raised_ref[:, pl.ds(base + start, PIECE)] = packed
        mix_ref[:, span] = dot_nn(values_t[...], packed)
        stat_ref[:, span] = jnp.where(row == 0, top, total)


def cross_open(block, low, high, partner, cross_project):
    chunk = partner.shape[0]
    half = low.shape[0]
    tokens = 2 * half
    steps = tokens // block
    row = lambda i: (i, 0)
    column = lambda i: (0, i)
    return pl.pallas_call(
        cross_open_kernel,
        grid=(steps,),
        in_specs=[
            pl.BlockSpec((block, D), lambda i: (jnp.minimum(i, steps // 2 - 1), 0)),
            pl.BlockSpec((block, D), lambda i: (jnp.maximum(i - steps // 2, 0), 0)),
            full_spec(partner.shape),
            full_spec(cross_project.shape),
        ],
        out_specs=[
            pl.BlockSpec((block, D), row),
            pl.BlockSpec((block, D), row),
            full_spec((chunk, 2 * D)),
            pl.BlockSpec((D, block), column),
            pl.BlockSpec((8, block), column),
            pl.BlockSpec(memory_space=pltpu.VMEM),
        ],
        out_shape=[
            jax.ShapeDtypeStruct((tokens, D), BF16),
            jax.ShapeDtypeStruct((tokens, D), BF16),
            jax.ShapeDtypeStruct((chunk, 2 * D), BF16),
            jax.ShapeDtypeStruct((D, tokens), F32),
            jax.ShapeDtypeStruct((8, tokens), F32),
            pltpu.VMEM((chunk, tokens), BF16),
        ],
        scratch_shapes=[pltpu.VMEM((D, chunk), BF16)],
        compiler_params=LOCAL_LIMIT,
        name="cross_open",
    )(low, high, partner, cross_project)


def cross_close_kernel(
    middle_ref, partner_ref, project_ref, q_ref, open_mix_ref, open_stat_ref,
    merge_ref, feed_in_ref, feed_out_ref, gains_ref, upstream_ref,
    kv_ref, result_ref, mid_grad_ref, mix_grad_ref, stat_ref,
    grad_in_ref, grad_out_ref, grad_merge_ref, grad_gain_ref, raised_ref,
    values_t, grad_out_t,
):
    step = pl.program_id(0)
    block = middle_ref.shape[0]

    @pl.when(step == 0)
    def _():
        kv_ref[...] = dot_nn(partner_ref[...], project_ref[:, D:]).astype(BF16)
        values_t[...] = kv_ref[:, D:].T
        grad_in_ref[...] = jnp.zeros_like(grad_in_ref)
        grad_out_t[...] = jnp.zeros_like(grad_out_t)
        grad_merge_ref[...] = jnp.zeros_like(grad_merge_ref)
        grad_gain_ref[...] = jnp.zeros_like(grad_gain_ref)

    base = pl.multiple_of(step * block, block)
    pieces, first_factors, second_factors = [], [], []
    logits = key_scores(kv_ref, q_ref[:PIECE, :])
    for start in range(0, block, PIECE):
        span = slice(start, start + PIECE)
        current = logits
        if start + PIECE < block:
            logits = key_scores(kv_ref, q_ref[start + PIECE : start + 2 * PIECE, :])
        open_top = open_stat_ref[0:1, span]
        top = jnp.maximum(jnp.max(current, axis=0, keepdims=True), open_top)
        raised = jnp.exp2(current - top)
        carry = jnp.exp2(open_top - top)
        total = jnp.sum(raised, axis=0, keepdims=True) + open_stat_ref[1:2, span] * carry
        packed = raised.astype(BF16)
        raised_ref[:, pl.ds(base + start, PIECE)] = packed
        inverse_total = 1.0 / total
        pieces.append(
            (dot_nn(values_t[...], packed) + open_mix_ref[:, span] * carry) * inverse_total
        )
        first_factors.append(carry * inverse_total)
        second_factors.append(inverse_total)
    mixed = jnp.concatenate(pieces, axis=1)
    first_factor = jnp.concatenate(first_factors, axis=1)
    second_factor = jnp.concatenate(second_factors, axis=1)
    mixed = mixed.T
    cross_mix = mixed.astype(BF16)

    middle = middle_ref[...]
    gain_cross = gains_ref[1:2, :]
    gain_feed = gains_ref[2:3, :]
    cross_full, cross_unit, cross_inverse = layer_norm(
        dot_nn(cross_mix, merge_ref[...]), gain_cross
    )
    cross_normed = cross_full.astype(BF16)
    feed_pre = dot_nn(middle, feed_in_ref[:D, :]) + dot_nn(cross_normed, feed_in_ref[D:, :])
    bell = 0.5 * (1.0 + lax.erf(feed_pre * HALF_ROOT))
    hidden = (feed_pre * bell).astype(BF16)
    slope = bell + feed_pre * (jnp.exp(-0.5 * feed_pre * feed_pre) * DENSITY_COEF)
    feed_normed, feed_unit, feed_inverse = layer_norm(
        dot_nn(hidden, feed_out_ref[...]), gain_feed
    )
    result_ref[...] = (middle.astype(F32) + feed_normed).astype(BF16)
    upstream = upstream_ref[...]
    post_full, gain_grad_feed = norm_backward(upstream, gain_feed, feed_unit, feed_inverse)
    grad_post = post_full.astype(BF16)
    grad_pre = (dot_nt(grad_post, feed_out_ref[...]) * slope).astype(BF16)
    grad_joined = dot_nt(grad_pre, feed_in_ref[...])
    mid_grad_ref[...] = upstream + grad_joined[:, :D]
    lanes = grad_in_ref.shape[0]
    grad_low = dot_tn(middle, grad_pre)
    grad_high = dot_tn(cross_normed, grad_pre)
    for b in range(lanes):
        grad_in_ref[b, :D, :] += grad_low[:, b * D : (b + 1) * D]
        grad_in_ref[b, D:, :] += grad_high[:, b * D : (b + 1) * D]
    grad_out_t[...] += dot_tn(grad_post, hidden)
    merged_full, gain_grad_cross = norm_backward(
        grad_joined[:, D:], gain_cross, cross_unit, cross_inverse
    )
    grad_merged = merged_full.astype(BF16)
    grad_merge_ref[...] += dot_tn(cross_mix, grad_merged)
    mix_grad = dot_nt(grad_merged, merge_ref[...]).astype(BF16)
    mix_grad_ref[...] = mix_grad
    inner = jnp.sum(mix_grad.astype(F32) * mixed, axis=-1, keepdims=True)
    inner_row = jnp.broadcast_to(inner, (block, D)).T[: stat_ref.shape[0], :]
    row = lax.broadcasted_iota(jnp.int32, stat_ref.shape, 0)
    stat_ref[...] = jnp.where(
        row == 0, inner_row, jnp.where(row == 1, first_factor, second_factor)
    )
    grad_gain_ref[1:2, :] += gain_grad_cross
    grad_gain_ref[2:3, :] += gain_grad_feed

    @pl.when(step == pl.num_programs(0) - 1)
    def _():
        grad_out_ref[...] = grad_out_t[...].T


def cross_close(
    block, middles, partner, cross_project, q, open_mix, open_stat,
    cross_merge, feed_in, feed_out, norm_gains, upstream,
):
    tokens = middles.shape[0]
    chunk = partner.shape[0]
    hidden = feed_in.shape[1]
    tile = pl.BlockSpec((block, D), lambda i: (i, 0))
    column = lambda i: (0, i)
    return pl.pallas_call(
        cross_close_kernel,
        grid=(tokens // block,),
        in_specs=[
            tile, full_spec(partner.shape), full_spec(cross_project.shape), tile,
            pl.BlockSpec((D, block), column), pl.BlockSpec((8, block), column),
            full_spec(cross_merge.shape), full_spec(feed_in.shape), full_spec(feed_out.shape),
            full_spec(norm_gains.shape), tile,
        ],
        out_specs=[
            full_spec((chunk, 2 * D)), tile, tile, tile,
            pl.BlockSpec((8, block), column),
            full_spec((hidden // D, 2 * D, D)), full_spec((hidden, D)), full_spec((D, D)),
            full_spec((8, D)),
            pl.BlockSpec(memory_space=pltpu.VMEM),
        ],
        out_shape=[
            jax.ShapeDtypeStruct((chunk, 2 * D), BF16),
            jax.ShapeDtypeStruct((tokens, D), BF16),
            jax.ShapeDtypeStruct((tokens, D), F32),
            jax.ShapeDtypeStruct((tokens, D), BF16),
            jax.ShapeDtypeStruct((8, tokens), F32),
            jax.ShapeDtypeStruct((hidden // D, 2 * D, D), F32),
            jax.ShapeDtypeStruct((hidden, D), F32),
            jax.ShapeDtypeStruct((D, D), F32),
            jax.ShapeDtypeStruct((8, D), F32),
            pltpu.VMEM((chunk, tokens), BF16),
        ],
        scratch_shapes=[pltpu.VMEM((D, chunk), BF16), pltpu.VMEM((D, hidden), F32)],
        compiler_params=LOCAL_LIMIT,
        name="cross_close",
    )(middles, partner, cross_project, q, open_mix, open_stat,
      cross_merge, feed_in, feed_out, norm_gains, upstream)


def cross_back_kernel(*refs, first, last, q_block, index, factor_row):
    refs = list(refs)
    q_ref, grad_ref, stat_ref, raised_ref, kv_ref, partner_ref, project_ref = refs[:7]
    refs = refs[7:]
    if not first:
        q_in_ref, weight_in_ref = refs[:2]
        refs = refs[2:]
    if last:
        mid_grad_ref, middle_ref = refs[:2]
        refs = refs[2:]
    term_ref, q_out_ref, weight_ref, k_acc, v_acc, q_acc = refs
    step = pl.program_id(0)

    @pl.when(step == 0)
    def _():
        if first:
            q_acc[...] = jnp.zeros_like(q_acc)
            weight_ref[...] = jnp.zeros_like(weight_ref)
        else:
            q_acc[...] = q_in_ref[...]
            weight_ref[...] = weight_in_ref[...]

    k_acc[...] = jnp.zeros_like(k_acc)
    v_acc[...] = jnp.zeros_like(v_acc)
    keys = kv_ref[:, :D]
    values = kv_ref[:, D:]
    tokens = q_ref.shape[0]
    block = kv_ref.shape[0]

    @pl.loop(0, tokens // q_block)
    def _(j):
        span = pl.ds(pl.multiple_of(j * q_block, q_block), q_block)
        q = q_ref[span, :]
        grad = grad_ref[span, :]
        inner = stat_ref[0:1, span]
        factor = stat_ref[factor_row : factor_row + 1, span]
        shares = raised_ref[index * block : (index + 1) * block, span].astype(F32) * factor
        slopes = dot_nt(values, grad) - inner
        v_acc[...] += dot_nn(shares.astype(BF16), grad)
        logit_grad = (shares * slopes).astype(BF16)
        k_acc[...] += dot_nn(logit_grad, q)
        q_acc[span, :] += dot_tn(logit_grad, keys)

    pair = jnp.concatenate(
        [(k_acc[...] * SCALE).astype(BF16), v_acc[...].astype(BF16)], axis=1
    )
    term_ref[...] = dot_nt(pair, project_ref[:, D:]).astype(BF16)
    pair_weight = dot_tn(partner_ref[...], pair)
    weight_ref[1] += pair_weight[:, :D]
    weight_ref[2] += pair_weight[:, D:]

    @pl.when(step == pl.num_programs(0) - 1)
    def _():
        if last:
            q_grad = (q_acc[...] * SCALE).astype(BF16)
            q_out_ref[...] = mid_grad_ref[...] + dot_nt(q_grad, project_ref[:, :D])
            weight_ref[0] += dot_tn(middle_ref[...], q_grad)
        else:
            q_out_ref[...] = q_acc[...]


def cross_back(
    block, index, factor_row, q_block, q, mix_grad, stats, raised, kv, partner, cross_project,
    carried=None, finish=None,
):
    tokens = q.shape[0]
    first, last = carried is None, finish is not None
    args = [q, mix_grad, stats, on_chip(raised), kv, partner, cross_project]
    specs = [
        full_spec(q.shape), full_spec(mix_grad.shape), full_spec(stats.shape),
        pl.BlockSpec(memory_space=pltpu.VMEM),
        pl.BlockSpec((block, 2 * D), lambda i: (index, 0)),
        pl.BlockSpec((block, D), lambda i: (index, 0)),
        full_spec(cross_project.shape),
    ]
    for extra in (carried or ()) + (finish or ()):
        args.append(extra)
        specs.append(full_spec(extra.shape))
    return pl.pallas_call(
        functools.partial(
            cross_back_kernel, first=first, last=last, q_block=q_block, index=index,
            factor_row=factor_row,
        ),
        grid=(1,),
        in_specs=specs,
        out_specs=[
            full_spec((block, D)), full_spec((tokens, D)), full_spec((3, D, D)),
        ],
        out_shape=[
            jax.ShapeDtypeStruct((block, D), BF16),
            jax.ShapeDtypeStruct((tokens, D), F32),
            jax.ShapeDtypeStruct((3, D, D), F32),
        ],
        scratch_shapes=[
            pltpu.VMEM((block, D), F32), pltpu.VMEM((block, D), F32), pltpu.VMEM((tokens, D), F32)
        ],
        compiler_params=LOCAL_LIMIT,
        name="cross_back",
    )(*args)


def self_back_kernel(
    offsets_ref, place_ref, own_ref, halo_ref, qkv_ref, halo_kv_ref, mix_ref, mid_grad_ref,
    term_low_ref, term_high_ref, project_ref, merge_ref, gains_ref,
    feature_grad_ref, halo_term_ref, weight_ref, merge_grad_ref, gain_ref,
    mix_grad, own_grad, halo_grad, own_back, halo_back,
    *, count, group,
):
    rows, cols = own_ref.shape[0], own_ref.shape[1]
    tokens = rows * cols
    offset, valid = whereabouts(offsets_ref, place_ref, count, group)
    forward, back = roll_matrices(offset, cols)
    upstream = mid_grad_ref[...] + jnp.concatenate(
        [term_low_ref[...].astype(F32), term_high_ref[...].astype(F32)], axis=0
    )
    gain = gains_ref[0:1, :]
    _, unit, inverse = layer_norm(dot_nn(mix_ref[...], merge_ref[...]), gain)
    merged_full, gain_grad = norm_backward(upstream, gain, unit, inverse)
    gain_row = lax.broadcasted_iota(jnp.int32, gain_ref.shape, 0)
    gain_ref[...] = jnp.where(gain_row == 0, gain_grad, 0.0)
    grad_merged = merged_full.astype(BF16)
    merge_grad_ref[...] = dot_tn(mix_ref[...], grad_merged)
    plain_grad = dot_nt(grad_merged, merge_ref[...]).astype(BF16)
    for r in range(rows):
        mix_grad[r] = dot_nn(forward, plain_grad[r * cols : (r + 1) * cols, :]).astype(BF16)
    for w in range(cols // WIN):
        span = slice(w * WIN, (w + 1) * WIN)
        q = pick(qkv_ref, span, slice(0, D))
        k_own = pick(qkv_ref, span, slice(D, 2 * D))
        k_halo = pick(halo_kv_ref, span, slice(0, D))
        grad = pick(mix_grad, span, slice(0, D))
        s_own = dot_nt(k_own, q) * SCALE
        s_halo = jnp.where(valid, dot_nt(k_halo, q) * SCALE, MASK_FILL)
        top = jnp.maximum(
            jnp.max(s_own, axis=0, keepdims=True), jnp.max(s_halo, axis=0, keepdims=True)
        )
        p_own = jnp.exp(s_own - top)
        p_halo = jnp.exp(s_halo - top)
        inv = 1.0 / (
            jnp.sum(p_own, axis=0, keepdims=True) + jnp.sum(p_halo, axis=0, keepdims=True)
        )
        p_own = p_own * inv
        p_halo = p_halo * inv
        d_own = dot_nt(pick(qkv_ref, span, slice(2 * D, 3 * D)), grad)
        d_halo = dot_nt(pick(halo_kv_ref, span, slice(D, 2 * D)), grad)
        inner = jnp.sum(p_own * d_own, axis=0, keepdims=True) + jnp.sum(
            p_halo * d_halo, axis=0, keepdims=True
        )
        l_own = (p_own * (d_own - inner) * SCALE).astype(BF16)
        l_halo = (p_halo * (d_halo - inner) * SCALE).astype(BF16)
        q_grad = dot_tn(l_own, k_own) + dot_tn(l_halo, k_halo)
        shape = (rows, WIN, D)
        own_grad[:, span, :D] = q_grad.astype(BF16).reshape(shape)
        own_grad[:, span, D : 2 * D] = dot_nn(l_own, q).astype(BF16).reshape(shape)
        own_grad[:, span, 2 * D :] = dot_nn(p_own.astype(BF16), grad).astype(BF16).reshape(shape)
        halo_grad[:, span, :D] = dot_nn(l_halo, q).astype(BF16).reshape(shape)
        halo_grad[:, span, D:] = dot_nn(p_halo.astype(BF16), grad).astype(BF16).reshape(shape)
    for r in range(rows):
        line = slice(r * cols, (r + 1) * cols)
        halo_back[line, :] = dot_nn(back, halo_grad[r]).astype(BF16)
        own_back[line, :] = dot_nn(back, own_grad[r]).astype(BF16)
    halo_term_ref[...] = dot_nt(halo_back[...], project_ref[:, D:]).astype(BF16)
    feature_grad_ref[...] = upstream + dot_nt(own_back[...], project_ref[...])
    own = own_ref[...].reshape(tokens, D)
    halo = halo_ref[...].reshape(tokens, D)
    own_weight = dot_tn(own, own_back[...])
    halo_weight = dot_tn(halo, halo_back[...])
    weight_ref[0] = own_weight[:, :D]
    weight_ref[1] = own_weight[:, D : 2 * D] + halo_weight[:, :D]
    weight_ref[2] = own_weight[:, 2 * D :] + halo_weight[:, D:]


def self_back(
    group, offsets, place, features, halo, qkv, halo_kv, mix, mid_grad, term_low, term_high,
    self_project, self_merge, norm_gains,
):
    rows, cols, _ = halo.shape
    tokens = rows * cols
    return pl.pallas_call(
        functools.partial(
            self_back_kernel, count=lax.axis_size("tiles"), group=group
        ),
        grid=(1,),
        in_specs=[
            pl.BlockSpec(memory_space=pltpu.SMEM),
            pl.BlockSpec(memory_space=pltpu.SMEM),
            pl.BlockSpec((rows, cols, D), lambda i: (group, 0, 0)),
            full_spec(halo.shape), full_spec(qkv.shape), full_spec(halo_kv.shape),
            full_spec(mix.shape),
            pl.BlockSpec((tokens, D), lambda i: (group, 0)),
            full_spec(term_low.shape), full_spec(term_high.shape),
            full_spec(self_project.shape), full_spec(self_merge.shape),
            full_spec(norm_gains.shape),
        ],
        out_specs=[
            full_spec((tokens, D)), full_spec((tokens, D)), full_spec((3, D, D)),
            full_spec((D, D)), full_spec((8, D)),
        ],
        out_shape=[
            jax.ShapeDtypeStruct((tokens, D), F32),
            jax.ShapeDtypeStruct((tokens, D), BF16),
            jax.ShapeDtypeStruct((3, D, D), F32),
            jax.ShapeDtypeStruct((D, D), F32),
            jax.ShapeDtypeStruct((8, D), F32),
        ],
        scratch_shapes=[
            pltpu.VMEM((rows, cols, D), BF16),
            pltpu.VMEM((rows, cols, 3 * D), BF16),
            pltpu.VMEM((rows, cols, 2 * D), BF16),
            pltpu.VMEM((tokens, 3 * D), BF16),
            pltpu.VMEM((tokens, 2 * D), BF16),
        ],
        compiler_params=LOCAL_LIMIT,
        name="self_back",
    )(offsets, place, features, halo, qkv, halo_kv, mix, mid_grad, term_low, term_high,
      self_project, self_merge, norm_gains)


def pack_kernel(
    place_ref, self_a, self_b, merge_a, merge_b, cross_ref, cross_merge_ref, in_ref, out_ref,
    gain_a, gain_b, gain_c, kept_ref, sent_ref,
):
    pairs = kept_ref.shape[0]
    odd = lax.rem(place_ref[0], 2)
    sources = [[self_a.at[b], self_b.at[b]] for b in range(self_a.shape[0])]
    sources += [[merge_a, merge_b]]
    sources += [[cross_ref.at[b]] for b in range(cross_ref.shape[0])]
    sources += [[cross_merge_ref]]
    sources += [[in_ref.at[b]] for b in range(in_ref.shape[0])]
    sources += [[out_ref]]
    gains = gain_a[...] + gain_b[...] + gain_c[...]
    for p in range(pairs):
        start = 0
        for refs in sources:
            size = refs[0].shape[0] // (2 * pairs)
            kept_rows = pl.ds(pl.multiple_of((2 * p + odd) * size, size), size)
            sent_rows = pl.ds(pl.multiple_of((2 * p + 1 - odd) * size, size), size)
            kept = refs[0][kept_rows, :]
            sent = refs[0][sent_rows, :]
            for ref in refs[1:]:
                kept = kept + ref[kept_rows, :]
                sent = sent + ref[sent_rows, :]
            kept_ref[p, start : start + size, :] = kept
            sent_ref[p, start : start + size, :] = sent.astype(BF16)
            start += size
        kept_ref[p, start : start + gains.shape[0], :] = gains
        sent_ref[p, start : start + gains.shape[0], :] = gains.astype(BF16)


def pack(count, place, *arrays):
    rows = sum(math.prod(a.shape[:-1]) for a in arrays) // count
    rows -= sum(math.prod(arrays[i].shape[:-1]) for i in (1, 3)) // count
    rows -= sum(math.prod(a.shape[:-1]) for a in arrays[-3:]) // count
    rows += arrays[-1].shape[0]
    shape = (count // 2, rows, D)
    whole = pl.BlockSpec(memory_space=pltpu.VMEM)
    return pl.pallas_call(
        pack_kernel,
        in_specs=[pl.BlockSpec(memory_space=pltpu.SMEM)] + [whole] * len(arrays),
        out_specs=[whole, whole],
        out_shape=[jax.ShapeDtypeStruct(shape, F32), jax.ShapeDtypeStruct(shape, BF16)],
        compiler_params=LOCAL_LIMIT,
        name="pack",
    )(place, *arrays)


def unpack_kernel(place_ref, kept_ref, got_ref, *outs, scale):
    start = 0
    for out in outs[:-1]:
        size = out.shape[0]
        for b in range(out.shape[1] // D):
            rows = slice(start, start + size)
            out[:, b * D : (b + 1) * D] = (
                kept_ref[0, rows, :] + got_ref[0, rows, :].astype(F32)
            ) * scale
            start += size
    gains_out = outs[-1]
    lanes = gains_out.shape[1]
    rows = slice(start, start + 8)
    gains = (kept_ref[0, rows, :] + got_ref[0, rows, :].astype(F32)) * scale
    shift = lax.rem(D - place_ref[0] * lanes, D)
    gains_out[...] = pltpu.roll(gains, shift, 1)[: gains_out.shape[0], :lanes]


def unpack(place, kept, got, shapes, scale):
    whole = pl.BlockSpec(memory_space=pltpu.VMEM)
    return pl.pallas_call(
        functools.partial(unpack_kernel, scale=scale),
        in_specs=[pl.BlockSpec(memory_space=pltpu.SMEM), whole, whole],
        out_specs=[whole] * len(shapes),
        out_shape=[jax.ShapeDtypeStruct(shape, F32) for shape in shapes],
        compiler_params=LOCAL_LIMIT,
        name="unpack",
    )(place, kept, got)


def scattered_halves(kept, sent, axis):
    count = lax.axis_size(axis)
    index = lax.axis_index(axis)
    bit = 1
    while True:
        got = lax.ppermute(sent, axis, [(i, i ^ bit) for i in range(count)])
        if kept.shape[0] == 1:
            return kept, got
        bit *= 2
        pairs = (kept + got.astype(F32)).reshape((kept.shape[0] // 2, 2) + kept.shape[1:])
        odd = (index & bit) != 0
        kept = jnp.where(odd, pairs[:, 1], pairs[:, 0])
        sent = jnp.where(odd, pairs[:, 0], pairs[:, 1]).astype(BF16)


def body(
    features, window_offsets, self_project, self_merge, cross_project, cross_merge,
    feed_in, feed_out, norm_gains, result_grad,
):
    tile_rows, tile_cols = features.shape[0], features.shape[1]
    half_rows = tile_rows // 2
    tile_tokens = tile_rows * tile_cols
    half_tokens = tile_tokens // 2
    count = lax.axis_size("tiles")
    half_tiles = count // 2
    shift = count // 4
    place = lax.axis_index("tiles").astype(jnp.int32).reshape(1)
    grad_scale = 1.0 / math.sqrt(count * tile_tokens)
    inner = [
        ((i + shift) % count, (i + 1 + shift) % count)
        for i in range(count)
        if i % half_tiles != half_tiles - 1
    ]
    to_next = inner
    to_previous = [(b, a) for a, b in inner]
    to_partner = [(i, (i + half_tiles) % count) for i in range(count)]

    raw_features = features
    features = off_chip(features)
    self_project, self_merge, cross_project, cross_merge, feed_in, feed_out, norm_gains = (
        off_chip(w)
        for w in (
            self_project, self_merge, cross_project, cross_merge, feed_in, feed_out, norm_gains
        )
    )
    halos = (
        lax.ppermute(raw_features[half_rows:], "tiles", to_next),
        lax.ppermute(raw_features[:half_rows], "tiles", to_previous),
    )
    parts = [
        self_forward(g, window_offsets, place, features, halos[g], self_project, self_merge, norm_gains)
        for g in range(2)
    ]
    partners = [lax.ppermute(parts[g][0], "tiles", to_partner) for g in range(2)]

    block = min(1024, half_tokens)
    upstream = off_chip(result_grad.reshape(tile_tokens, D))
    middles, q, kv_a, open_mix, open_stat, raised_a = cross_open(
        block, parts[0][0], parts[1][0], partners[0], cross_project
    )
    (kv_b, result, mid_grad, mix_grad, stats, grad_in, grad_out, grad_merge, gain_grad,
     raised_b) = (
        cross_close(
            block, middles, partners[1], cross_project, q, open_mix, open_stat,
            cross_merge, feed_in, feed_out, norm_gains, upstream,
        )
    )
    half = half_tokens // 2
    carried, got = None, []
    for c in range(4):
        term, q_grad, cross_weight = cross_back(
            half, c % 2, 1 + c // 2, half, q, mix_grad, stats,
            (raised_a, raised_b)[c // 2], (kv_a, kv_b)[c // 2],
            partners[c // 2], cross_project,
            carried=carried, finish=(mid_grad, middles) if c == 3 else None,
        )
        carried = (q_grad, cross_weight)
        got.append(lax.ppermute(term, "tiles", to_partner))
    mid_grad = q_grad
    backs, terms = [], []
    for g in range(2):
        backs.append(
            self_back(
                g, window_offsets, place, features, halos[g],
                on_chip(parts[g][2]), on_chip(parts[g][3]), on_chip(parts[g][1]),
                mid_grad, got[2 * g], got[2 * g + 1], self_project, self_merge, norm_gains,
            )
        )
        terms.append(
            lax.ppermute(backs[g][1], "tiles", (to_previous, to_next)[g])
        )
    from_next, from_previous = terms
    features_grad = jnp.concatenate(
        [
            backs[0][0] + from_previous.astype(F32),
            backs[1][0] + from_next.astype(F32),
        ],
        axis=0,
    ).reshape(tile_rows, tile_cols, D)

    kept, got_last = scattered_halves(
        *pack(
            count, place, backs[0][2], backs[1][2], backs[0][3], backs[1][3], cross_weight,
            grad_merge, grad_in, grad_out, backs[0][4], backs[1][4], gain_grad,
        ),
        "tiles",
    )
    grads = unpack(
        place, kept, got_last,
        [
            (D // count, 3 * D), (D // count, D), (D // count, 3 * D), (D // count, D),
            (2 * D // count, feed_in.shape[1]), (feed_out.shape[0] // count, D),
            (norm_gains.shape[0], D // count),
        ],
        grad_scale,
    )
    return (
        result.reshape(tile_rows, tile_cols, D),
        features_grad,
        *grads,
    )


def solution(mesh):
    whole = P(("groups", "tiles"), None, None)
    rows = P(("groups", "tiles"), None)
    return jax.shard_map(
        body,
        mesh=mesh,
        in_specs=(whole, P("groups"), P(), P(), P(), P(), P(), P(), P(), whole),
        out_specs=(whole, whole, rows, rows, rows, rows, rows, rows, P("groups", "tiles")),
        check_vma=False,
    )
```
